128 devices in a mesh: row: 8 (over x, y_hi), col: 16 (over y_lo, z, core).
Axes of the slice: x: 4, y: 4 (y_hi: 2, y_lo: 2; y = y_hi * 2 + y_lo), z: 4, core: 2. Of those that a mesh axis runs over, the one named last changes fastest.
Arguments:
- tokens: bfloat16 [768, 8192], P('row', 'col'), may hold values from -6 to 6
- weight_in: bfloat16 [8192, 32768], P('col', 'row'), may hold values from -0.125 to 0.125
- mask_in: int32 [64, 256], P('col', 'row'), may hold values 0 or 1
- weight_out: bfloat16 [32768, 8192], P('row', 'col'), may hold values from -0.0625 to 0.0625
- mask_out: int32 [256, 64], P('row', 'col'), may hold values 0 or 1
- cotangent: bfloat16 [768, 8192], P('row', 'col'), may hold values from -6 to 6
Outputs:
- result: bfloat16 [768, 8192], P('row', 'col')
- tokens_grad: bfloat16 [768, 8192], P('row', 'col')
- weight_in_grad: bfloat16 [8192, 32768], P('col', 'row')
- weight_out_grad: bfloat16 [32768, 8192], P('row', 'col')
The draws below stay inside these ranges and needn't reach their ends.
All inputs are finite; a program needn't handle non-finite values. No bound on the sum of `mask_in` or of `mask_out` on one device may be relied on, other than what follows from the above.
Results may differ from the reference program's by a relative error of at most 0.005.
Values may be sent and summed in bfloat16 or wider, within the bound.
A program may use at most 128 MiB of HBM per device.

```python
import jax
import jax.numpy as jnp

D = 8192
FF = 32768
BLOCK = 128
TOKENS = 768


def set_ends(drawn, stream_key, least, high):
    spot = [jax.random.randint(jax.random.fold_in(stream_key, axis), (), 0, length) for axis, length in enumerate(drawn.shape)]
    widest = drawn.shape.index(max(drawn.shape))
    next_to = spot[:widest] + [(spot[widest] + 1) % drawn.shape[widest]] + spot[widest + 1:]
    return drawn.at[tuple(spot)].set(least).at[tuple(next_to)].set(high)


def levels(own_key, shape, cuts, low, largest):
    loudness, own = 1.0, jax.random.fold_in(own_key, 6)
    for axis_at, parts in cuts:
        heights = jnp.exp(jax.random.uniform(jax.random.fold_in(own, axis_at), (parts,), jnp.float32, low / len(cuts), largest / len(cuts)))
        loudness = loudness * jnp.repeat(heights, shape[axis_at] // parts).reshape([-1 if axis == axis_at else 1 for axis in range(len(shape))])
    return loudness


def gaussian(own_key, dims, deviation, most, split=(), dtype=jnp.bfloat16):
    values = deviation * jax.random.normal(own_key, dims, jnp.float32)
    if split:
        values = values * levels(own_key, dims, split, -0.22, 0.18)
    return jnp.clip(values, -most, most).astype(dtype)


def setup_inputs(seed: int = 0) -> dict:
    key_list = jax.random.split(jax.random.key(seed), 7)
    tokens = gaussian(key_list[0], (TOKENS, D), 1.0, 6.0, ((0, 8), (1, 16)))
    weight_in = gaussian(key_list[1], (D, FF), (D // 4) ** -0.5, 0.125, ((0, 16), (1, 8)))
    mask_in = set_ends((jax.random.randint(key_list[2], (D // BLOCK, FF // BLOCK), 0, 4) < 1).astype(jnp.int32), jax.random.fold_in(key_list[2], 1), 0, 1)
    weight_out = gaussian(key_list[3], (FF, D), (FF // 4) ** -0.5, 0.0625, ((0, 8), (1, 16)))
    mask_out = set_ends((jax.random.randint(key_list[4], (FF // BLOCK, D // BLOCK), 0, 4) < 1).astype(jnp.int32), jax.random.fold_in(key_list[4], 1), 0, 1)
    cotangent = gaussian(key_list[5], (TOKENS, D), 1.0, 6.0, ((0, 8), (1, 16)))
    return dict(tokens=tokens, weight_in=weight_in, mask_in=mask_in, weight_out=weight_out, mask_out=mask_out, cotangent=cotangent)


root_two_pi = 0.7978845608
cubic_coef = 0.044715


def expand(mask):
    blocks_a, blocks_b = mask.shape
    spread = mask.astype(jnp.bfloat16)
    return jnp.broadcast_to(spread[:, None, :, None], (blocks_a, BLOCK, blocks_b, BLOCK)).reshape(blocks_a * BLOCK, blocks_b * BLOCK)


def gelu_value(values):
    tangent = jnp.tanh(root_two_pi * (values + cubic_coef * values * values * values))
    return 0.5 * values * (1.0 + tangent)


def gelu_slope(values):
    tangent = jnp.tanh(root_two_pi * (values + cubic_coef * values * values * values))
    return 0.5 * (1.0 + tangent) + 0.5 * values * (1.0 - tangent * tangent) * root_two_pi * (1.0 + 3.0 * cubic_coef * values * values)


def reference(tokens, weight_in, mask_in, weight_out, mask_out, cotangent):
    block_in = expand(mask_in)
    block_out = expand(mask_out)
    masked_in = weight_in * block_in
    masked_out = weight_out * block_out
    preact = jnp.dot(tokens, masked_in, preferred_element_type=jnp.float32)
    hidden = gelu_value(preact).astype(jnp.bfloat16)
    result = jnp.dot(hidden, masked_out, preferred_element_type=jnp.float32).astype(jnp.bfloat16)
    hidden_grad = jnp.dot(cotangent, masked_out.T, preferred_element_type=jnp.float32)
    preact_grad = (hidden_grad * gelu_slope(preact)).astype(jnp.bfloat16)
    tokens_grad = jnp.dot(preact_grad, masked_in.T, preferred_element_type=jnp.float32).astype(jnp.bfloat16)
    weight_in_grad = (jnp.dot(tokens.T, preact_grad, preferred_element_type=jnp.float32) * block_in).astype(jnp.bfloat16)
    weight_out_grad = (jnp.dot(hidden.T, cotangent, preferred_element_type=jnp.float32) * block_out).astype(jnp.bfloat16)
    return result, tokens_grad, weight_in_grad, weight_out_grad
```

```python
import jax
import jax.numpy as jnp
from jax import lax
from jax.experimental import pallas as pl
from jax.experimental.pallas import tpu as pltpu
from jax.sharding import PartitionSpec as P

BLOCK = 128
CHUNKS = 8
WIDE = 256
BF = jnp.bfloat16
F32 = jnp.float32

root_two_pi = 0.7978845608
cubic_coef = 0.044715

ORDERS = ((0, 2, 1), (1, 2, 0), (2, 0, 1), (0, 1, 2), (1, 0, 2), (2, 1, 0), (0, 2, 1), (1, 2, 0))


def dot(left, right, left_dim, right_dim):
    return lax.dot_general(
        left, right, (((left_dim,), (right_dim,)), ((), ())), preferred_element_type=F32
    )


def gelu_both(values):
    tangent = jnp.tanh(root_two_pi * (values + cubic_coef * values * values * values))
    value = 0.5 * values * (1.0 + tangent)
    slope = 0.5 * (1.0 + tangent) + 0.5 * values * (1.0 - tangent * tangent) * root_two_pi * (
        1.0 + 3.0 * cubic_coef * values * values
    )
    return value, slope


N_COPIES = 160


def kernel(
    tok, cot, win, wout, mi, mo,
    res_o, tg_o, dwi_o, dwo_o,
    TA, CA, WI, WO, SI, SO,
    S1a, R1a, ACa, S2a, R2a, S3a, R3a,
    S1b, R1b, ACb, S2b, R2b, S3b, R3b,
    H, G, R, RX, T1, U1, T2, U2, T3, U3, OUT,
    send_sem, recv_sem, local_sem,
):
    row = lax.axis_index("row")
    col = lax.axis_index("col")
    x, yh = lax.div(row, 2), lax.rem(row, 2)
    yl = lax.div(col, 8)
    z = lax.div(lax.rem(col, 8), 2)
    core = lax.rem(col, 2)
    xb, xa = lax.div(x, 2), lax.rem(lax.div(x + 1, 2), 2)
    zb, za = lax.div(z, 2), lax.rem(lax.div(z + 1, 2), 2)
    here = {"row": row, "col": col}
    at_core = {"row": row, "col": col + 1 - 2 * core}
    at_y = {"row": row, "col": col + 8 - 16 * yl}
    at_za = {"row": row, "col": col + 2 * (1 - 2 * lax.rem(z, 2))}
    at_zb = {"row": row, "col": col + 2 * (3 - 2 * z)}
    at_xa = {"row": row + 2 * (1 - 2 * lax.rem(x, 2)), "col": col}
    at_xb = {"row": row + 2 * (3 - 2 * x), "col": col}
    at_yh = {"row": row + 1 - 2 * yh, "col": col}
    del here
    bits = (yl, za, zb)
    partner = (at_y, at_za, at_zb)

    count = [0]
    sent = []

    def push(src, dst, where):
        k = count[0]
        count[0] += 1
        copy = pltpu.make_async_remote_copy(
            src_ref=src, dst_ref=dst, send_sem=send_sem.at[k], recv_sem=recv_sem.at[k],
            device_id=where, device_id_type=pl.DeviceIdType.MESH,
        )
        copy.start()
        sent.append(copy)
        return copy

    lcount = [0]

    def local(src, dst):
        k = lcount[0]
        lcount[0] += 1
        copy = pltpu.make_async_copy(src, dst, local_sem.at[k])
        copy.start()
        return copy

    tok_in = local(tok, TA.at[core, xb, xa, yh])
    cot_in = local(cot, CA.at[core, xb, xa, yh])
    si_in = [local(win.at[:, pl.ds(h * 2048, 2048)], SI.at[h]) for h in range(2)]
    so_in = [local(wout.at[pl.ds(h * 2048, 2048)], SO.at[h]) for h in range(2)]

    barrier = pltpu.get_barrier_semaphore()
    for where in (at_core, at_y, at_za, at_zb, at_xa, at_xb, at_yh):
        pl.semaphore_signal(barrier, inc=1, device_id=where, device_id_type=pl.DeviceIdType.MESH)
    pl.semaphore_wait(barrier, 7)

    def gather_first(A):
        c = {}
        c["y"] = push(A.at[core, xb, xa, yh], A.at[core, xb, xa, yh], at_yh)
        c["a0"] = push(A.at[core, xb, xa, yh, 0], A.at[core, xb, xa, yh, 0], at_xb)
        c["b0"] = push(A.at[core, xb, xa, yh, 1], A.at[core, xb, xa, yh, 1], at_xa)
        return c

    def gather_second(A, c, v, tag):
        c["a" + tag].wait_recv()
        c["A" + tag] = push(A.at[core, :, xa, v, 0], A.at[core, :, xa, v, 0], at_xa)
        c["b" + tag].wait_recv()
        c["B" + tag] = push(A.at[core, xb, :, v, 1], A.at[core, xb, :, v, 1], at_xb)

    def gather_third(A, c, v):
        c["y"].wait_recv()
        c["a1"] = push(A.at[core, xb, xa, v, 0], A.at[core, xb, xa, v, 0], at_xb)
        c["b1"] = push(A.at[core, xb, xa, v, 1], A.at[core, xb, xa, v, 1], at_xa)

    def gather_cross(A, c, v, tag):
        c["A" + tag].wait_recv()
        c["B" + tag].wait_recv()
        c["c" + tag] = push(A.at[core, :, :, v], A.at[core, :, :, v], at_core)

    tok_in.wait()
    tc = gather_first(TA)
    cot_in.wait()
    cc = gather_first(CA)

    other = 1 - core

    def mask_in_half(h, dst):
        def step(i, carry):
            r = pl.multiple_of(i * BLOCK, BLOCK)
            m = mi[i, :, pl.ds(pl.multiple_of(h * 2048, 2048), 2048)]
            w = SI[h, pl.ds(r, BLOCK), :].reshape(8, 16, 2048)
            dst[pl.ds(r, BLOCK), :] = (w * m[None]).reshape(BLOCK, 2048)
            return carry
        lax.fori_loop(0, 4, step, 0)

    def mask_out_half(h, dst):
        def step(i, carry):
            r = pl.multiple_of(i * BLOCK, BLOCK)
            m = mo[h * 16 + i]
            w = SO[h, pl.ds(r, BLOCK), :].reshape(8, 16, 512)
            dst[pl.ds(r, BLOCK), :] = (w * m[None]).reshape(BLOCK, 512)
            return carry
        lax.fori_loop(0, 16, step, 0)

    for c in si_in:
        c.wait()
    mask_in_half(other, SI.at[other])
    wi_c = push(SI.at[other], WI.at[core], at_core)
    gather_second(TA, tc, yh, "0")
    gather_third(TA, tc, 1 - yh)
    mask_in_half(core, WI.at[core])
    for c in so_in:
        c.wait()
    mask_out_half(other, SO.at[other])
    wo_c = push(SO.at[other], WO.at[core], at_core)
    gather_second(TA, tc, 1 - yh, "1")
    gather_cross(TA, tc, yh, "0")
    gather_second(CA, cc, yh, "0")
    gather_third(CA, cc, 1 - yh)
    mask_out_half(core, WO.at[core])
    gather_cross(TA, tc, 1 - yh, "1")
    gather_second(CA, cc, 1 - yh, "1")
    wi_c.wait_recv()
    tc["c0"].wait_recv()
    tc["c1"].wait_recv()

    def part_in(j, half):
        out = None
        for k in range(2):
            t = dot(TA[k, half].reshape(384, 512), WI[k, :, WIDE * j : WIDE * (j + 1)], 1, 0)
            out = t if out is None else out + t
        return out.reshape(4, 96, WIDE)

    def part_out(j, half):
        out = None
        for k in range(2):
            t = dot(CA[k, half].reshape(384, 512), WO[k, WIDE * j : WIDE * (j + 1), :], 1, 1)
            out = t if out is None else out + t
        return out.reshape(4, 96, WIDE)

    streams = ((part_in, S1a, R1a, ACa, S2a, R2a, S3a, R3a), (part_out, S1b, R1b, ACb, S2b, R2b, S3b, R3b))
    first = [[None] * CHUNKS for _ in range(2)]
    second = [[None] * CHUNKS for _ in range(2)]
    third = [[None] * CHUNKS for _ in range(2)]

    def halve_first(s, j):
        part, S1, R1, AC, S2, R2, S3, R3 = streams[s]
        d = ORDERS[j][0]
        S1[j] = part(j, 1 - bits[d]).astype(BF)
        first[s][j] = push(S1.at[j], R1.at[j], partner[d])

    def halve_kept(s, j):
        part, S1, R1, AC, S2, R2, S3, R3 = streams[s]
        AC[j] = part(j, bits[ORDERS[j][0]])

    def halve_second(s, j):
        part, S1, R1, AC, S2, R2, S3, R3 = streams[s]
        d = ORDERS[j][1]
        away, keep = 2 * (1 - bits[d]), 2 * bits[d]
        first[s][j].wait_recv()
        S2[j] = (AC[j, pl.ds(away, 2)] + R1[j, pl.ds(away, 2)].astype(F32)).astype(BF)
        second[s][j] = push(S2.at[j], R2.at[j], partner[d])
        AC[j, pl.ds(keep, 2)] = AC[j, pl.ds(keep, 2)] + R1[j, pl.ds(keep, 2)].astype(F32)

    def halve_third(s, j):
        part, S1, R1, AC, S2, R2, S3, R3 = streams[s]
        base, d = 2 * bits[ORDERS[j][1]], ORDERS[j][2]
        away, keep = 1 - bits[d], bits[d]
        second[s][j].wait_recv()
        S3[j] = (AC[j, base + away] + R2[j, away].astype(F32)).astype(BF)
        third[s][j] = push(S3.at[j], R3.at[j], partner[d])
        AC[j, base + keep] = AC[j, base + keep] + R2[j, keep].astype(F32)

    def whole(s, j):
        part, S1, R1, AC, S2, R2, S3, R3 = streams[s]
        third[s][j].wait_recv()
        q = 2 * bits[ORDERS[j][1]] + bits[ORDERS[j][2]]
        return AC[j, q] + R3[j].astype(F32), q

    d1 = [[None] * CHUNKS for _ in range(2)]
    d2 = [[None] * CHUNKS for _ in range(2)]
    d3 = [[None] * CHUNKS for _ in range(2)]

    def double_first(s, j, A):
        m = [bits[d] for d in ORDERS[j]]
        at = A.at[j, 4 * m[0] + 2 * m[1] + m[2]]
        d1[s][j] = push(at, at, partner[ORDERS[j][2]])

    def double_second(s, j, A):
        m = [bits[d] for d in ORDERS[j]]
        d1[s][j].wait_recv()
        at = A.at[j, pl.ds(4 * m[0] + 2 * m[1], 2)]
        d2[s][j] = push(at, at, partner[ORDERS[j][1]])

    def double_third(s, j, A):
        m = [bits[d] for d in ORDERS[j]]
        d2[s][j].wait_recv()
        at = A.at[j, pl.ds(4 * m[0], 4)]
        d3[s][j] = push(at, at, partner[ORDERS[j][0]])

    def make_hidden(j):
        m = [bits[d] for d in ORDERS[j]]
        v, q = whole(0, j)
        value, slope = gelu_both(v)
        H[j, 4 * m[0] + 2 * m[1] + m[2]] = value.astype(BF)
        ACa[j, q] = slope
        double_first(0, j, H)

    def make_grad(j):
        m = [bits[d] for d in ORDERS[j]]
        v, q = whole(1, j)
        G[j, 4 * m[0] + 2 * m[1] + m[2]] = (v * ACa[j, q]).astype(BF)
        double_first(1, j, G)

    each = range(CHUNKS)
    for j in each:
        halve_first(0, j)
    gather_cross(CA, cc, yh, "0")
    for j in each:
        halve_kept(0, j)
    gather_cross(CA, cc, 1 - yh, "1")
    wo_c.wait_recv()
    cc["c0"].wait_recv()
    cc["c1"].wait_recv()
    for j in each:
        halve_first(1, j)
    for j in each:
        halve_second(0, j)
    for j in each:
        halve_kept(1, j)
    for j in each:
        halve_third(0, j)
    for j in each:
        halve_second(1, j)
    for j in each:
        make_hidden(j)
    for j in each:
        halve_third(1, j)
    for j in each:
        double_second(0, j, H)
    for j in each:
        make_grad(j)
    for j in each:
        double_third(0, j, H)
    for j in each:
        double_second(1, j, G)

    def out_part(A, group, weight_of, right_dim):
        def step(t, carry):
            k, h = lax.div(t, 2), lax.rem(t, 2)
            left = jnp.concatenate(
                [A[4 * group + i, pl.ds(4 * h, 4)].reshape(384, WIDE) for i in range(4)], axis=1
            )
            got = dot(left, weight_of(k), 1, right_dim).reshape(2, 2, 2, 48, 512)
            if group == 0:
                R[k, h] = got
            else:
                R[k, h] = R[k, h] + got
            return carry
        lax.fori_loop(0, 4, step, 0)

    def row_cross(n):
        return push(R.at[other], RX.at[n], at_core)

    def full(n, idx):
        return R[(core,) + idx] + RX[(n,) + idx]

    def row_first(cross, n):
        cross.wait_recv()
        every = slice(None)
        T1[n, 0] = full(n, (1 - xb, every, every, 0)).astype(BF)
        a = push(T1.at[n, 0], U1.at[n, 0], at_xb)
        T1[n, 1] = full(n, (every, 1 - xa, every, 1)).astype(BF)
        b = push(T1.at[n, 1], U1.at[n, 1], at_xa)
        return a, b

    def row_second(copies, n):
        every = slice(None)
        copies[0].wait_recv()
        T2[n, 0] = (full(n, (xb, 1 - xa, every, 0)) + U1[n, 0, 1 - xa].astype(F32)).astype(BF)
        a = push(T2.at[n, 0], U2.at[n, 0], at_xa)
        copies[1].wait_recv()
        T2[n, 1] = (full(n, (1 - xb, xa, every, 1)) + U1[n, 1, 1 - xb].astype(F32)).astype(BF)
        b = push(T2.at[n, 1], U2.at[n, 1], at_xb)
        return a, b

    def row_sum(n, v, hf):
        near = (xa, xb)[hf]
        return full(n, (xb, xa, v, hf)) + U1[n, hf, near, v].astype(F32) + U2[n, hf, v].astype(F32)

    def row_third(copies, n):
        copies[0].wait_recv()
        T3[n, 0] = row_sum(n, 1 - yh, 0).astype(BF)
        copies[1].wait_recv()
        T3[n, 1] = row_sum(n, 1 - yh, 1).astype(BF)
        return push(T3.at[n], U3.at[n], at_yh)

    def row_last(copy, n, out):
        copy.wait_recv()
        for hf in range(2):
            OUT[n, hf] = (row_sum(n, yh, hf) + U3[n, hf].astype(F32)).astype(BF)
        return local(OUT.at[n], out)

    def out_grad(lo, hi):
        def step(j, carry):
            left = H[j].reshape(768, WIDE)
            for k in range(2):
                got = dot(left, CA[k].reshape(768, 512), 0, 0)
                SO[k, pl.ds(pl.multiple_of(j * WIDE, WIDE), WIDE), :] = got.astype(BF)
            return carry
        lax.fori_loop(lo, hi, step, 0)

    def in_grad():
        def step(t, carry):
            k, i = lax.div(t, 2), lax.rem(t, 2)
            d = pl.multiple_of(i * WIDE, WIDE)
            left = TA[k, :, :, :, :, :, pl.ds(d, WIDE)].reshape(768, WIDE)
            for j in range(CHUNKS):
                got = dot(left, G[j].reshape(768, WIDE), 0, 0)
                SI[k, pl.ds(d, WIDE), WIDE * j : WIDE * (j + 1)] = got.astype(BF)
            return carry
        lax.fori_loop(0, 4, step, 0)

    def wout_of(group):
        return lambda k: WO[k, 1024 * group : 1024 * (group + 1), :]

    def win_of(group):
        return lambda k: WI[k, :, 1024 * group : 1024 * (group + 1)]

    for j in range(4):
        d3[0][j].wait_recv()
    out_part(H, 0, wout_of(0), 0)
    for j in range(4, 8):
        d3[0][j].wait_recv()
    out_part(H, 1, wout_of(1), 0)
    cross0 = row_cross(0)
    for j in each:
        double_third(1, j, G)
    wo_c.wait_send()
    out_grad(0, 2)
    pair = row_first(cross0, 0)
    out_grad(2, 5)
    pair = row_second(pair, 0)
    out_grad(5, 8)
    cols = pl.ds(pl.multiple_of(core * 2048, 2048), 2048)
    dwo_far = push(SO.at[other], dwo_o.at[cols], at_core)
    dwo_own = local(SO.at[core], dwo_o.at[cols])
    last = row_third(pair, 0)
    out0 = row_last(last, 0, res_o)

    cross0.wait_send()
    for j in range(4):
        d3[1][j].wait_recv()
    out_part(G, 0, win_of(0), 1)
    for j in range(4, 8):
        d3[1][j].wait_recv()
    out_part(G, 1, win_of(1), 1)
    cross = row_cross(1)
    wi_c.wait_send()
    pair = row_first(cross, 1)
    in_grad()
    dwi_far = push(SI.at[other], dwi_o.at[:, cols], at_core)
    dwi_own = local(SI.at[core], dwi_o.at[:, cols])
    pair = row_second(pair, 1)
    last = row_third(pair, 1)
    out1 = row_last(last, 1, tg_o)
    dwo_far.wait_recv()
    dwi_far.wait_recv()
    for c in (out0, out1, dwo_own, dwi_own):
        c.wait()
    for c in sent:
        if c is not wo_c and c is not wi_c and c is not cross0:
            c.wait_send()


def body(tokens, weight_in, mask_in, weight_out, mask_out, cotangent):
    mi = jnp.broadcast_to(jnp.repeat(mask_in.astype(BF), BLOCK, axis=1)[:, None], (4, 16, 4096))
    mo = jnp.broadcast_to(jnp.repeat(mask_out.astype(BF), BLOCK, axis=1)[:, None], (32, 16, 512))
    anywhere = pl.BlockSpec(memory_space=pl.ANY)
    vmem = pl.BlockSpec(memory_space=pltpu.VMEM)

    def halving():
        return [
            pltpu.VMEM((CHUNKS, 4, 96, WIDE), BF),
            pltpu.VMEM((CHUNKS, 4, 96, WIDE), BF),
            pltpu.VMEM((CHUNKS, 4, 96, WIDE), F32),
            pltpu.VMEM((CHUNKS, 2, 96, WIDE), BF),
            pltpu.VMEM((CHUNKS, 2, 96, WIDE), BF),
            pltpu.VMEM((CHUNKS, 96, WIDE), BF),
            pltpu.VMEM((CHUNKS, 96, WIDE), BF),
        ]

    result, tokens_grad, dwi, dwo = pl.pallas_call(
        kernel,
        out_shape=(
            jax.ShapeDtypeStruct((2, 48, 512), BF),
            jax.ShapeDtypeStruct((2, 48, 512), BF),
            jax.ShapeDtypeStruct((512, 4096), BF),
            jax.ShapeDtypeStruct((4096, 512), BF),
        ),
        in_specs=[anywhere] * 4 + [vmem] * 2,
        out_specs=(anywhere,) * 4,
        scratch_shapes=[
            pltpu.VMEM((2, 2, 2, 2, 2, 48, 512), BF),
            pltpu.VMEM((2, 2, 2, 2, 2, 48, 512), BF),
            pltpu.VMEM((2, 512, 2048), BF),
            pltpu.VMEM((2, 2048, 512), BF),
            pltpu.VMEM((2, 512, 2048), BF),
            pltpu.VMEM((2, 2048, 512), BF),
        ]
        + halving()
        + halving()
        + [
            pltpu.VMEM((CHUNKS, 8, 96, WIDE), BF),
            pltpu.VMEM((CHUNKS, 8, 96, WIDE), BF),
            pltpu.VMEM((2, 2, 2, 2, 2, 48, 512), F32),
            pltpu.VMEM((2, 2, 2, 2, 2, 48, 512), F32),
            pltpu.VMEM((2, 2, 2, 2, 48, 512), BF),
            pltpu.VMEM((2, 2, 2, 2, 48, 512), BF),
            pltpu.VMEM((2, 2, 2, 48, 512), BF),
            pltpu.VMEM((2, 2, 2, 48, 512), BF),
            pltpu.VMEM((2, 2, 48, 512), BF),
            pltpu.VMEM((2, 2, 48, 512), BF),
            pltpu.VMEM((2, 2, 48, 512), BF),
            pltpu.SemaphoreType.DMA((N_COPIES,)),
            pltpu.SemaphoreType.DMA((N_COPIES,)),
            pltpu.SemaphoreType.DMA((16,)),
        ],
        compiler_params=pltpu.CompilerParams(
            collective_id=0, has_side_effects=True, vmem_limit_bytes=67043328
        ),
    )(tokens.reshape(2, 48, 512), cotangent.reshape(2, 48, 512), weight_in, weight_out, mi, mo)
    dwi = (dwi.reshape(4, 8, 16, 4096) * mi[:, None]).reshape(512, 4096)
    dwo = (dwo.reshape(32, 8, 16, 512) * mo[:, None]).reshape(4096, 512)
    return result.reshape(96, 512), tokens_grad.reshape(96, 512), dwi, dwo


def solution(mesh):
    return jax.shard_map(
        body,
        mesh=mesh,
        in_specs=(
            P("row", "col"),
            P("col", "row"),
            P("col", "row"),
            P("row", "col"),
            P("row", "col"),
            P("row", "col"),
        ),
        out_specs=(P("row", "col"), P("row", "col"), P("col", "row"), P("row", "col")),
        check_vma=False,
    )
```

```python
import jax
import jax.numpy as jnp
from jax import lax
from jax.experimental import pallas as pl
from jax.experimental.pallas import tpu as pltpu
from jax.sharding import PartitionSpec as P

BLOCK = 128
CHUNKS = 8
WIDE = 256
BF = jnp.bfloat16
F32 = jnp.float32

root_two_pi = 0.7978845608
cubic_coef = 0.044715

ORDERS = ((0, 2, 1), (1, 2, 0), (2, 0, 1), (0, 1, 2), (1, 0, 2), (2, 1, 0), (0, 2, 1), (1, 2, 0))


def dot(left, right, left_dim, right_dim):
    return lax.dot_general(
        left, right, (((left_dim,), (right_dim,)), ((), ())), preferred_element_type=F32
    )


def gelu_both(values):
    tangent = jnp.tanh(root_two_pi * (values + cubic_coef * values * values * values))
    value = 0.5 * values * (1.0 + tangent)
    slope = 0.5 * (1.0 + tangent) + 0.5 * values * (1.0 - tangent * tangent) * root_two_pi * (
        1.0 + 3.0 * cubic_coef * values * values
    )
    return value, slope
OUT_KIND = pltpu.VMEM
VMEM_BYTES = 49 * 1024 * 1024


N_COPIES = 192


def kernel(
    tok, cot, win, wout, mask_in, mask_out_t,
    res_o, tg_o, DI, DO,
    TA, CA, WI, WO, FI, FO, MIS, MI, MOS, MO,
    S1a, R1a, ACa, S2a, R2a, S3a, R3a,
    S1b, R1b, ACb, S2b, R2b, S3b, R3b,
    H, G, R, RX, T1, U1, T2, U2, T3, U3, KEEP,
    send_sem, recv_sem, local_sem,
):
    row = lax.axis_index("row")
    col = lax.axis_index("col")
    x, yh = lax.div(row, 2), lax.rem(row, 2)
    yl = lax.div(col, 8)
    z = lax.div(lax.rem(col, 8), 2)
    core = lax.rem(col, 2)
    other = 1 - core
    xb, xa = lax.div(x, 2), lax.rem(lax.div(x + 1, 2), 2)
    zb, za = lax.div(z, 2), lax.rem(lax.div(z + 1, 2), 2)
    at_core = {"row": row, "col": col + 1 - 2 * core}
    at_y = {"row": row, "col": col + 8 - 16 * yl}
    at_za = {"row": row, "col": col + 2 * (1 - 2 * lax.rem(z, 2))}
    at_zb = {"row": row, "col": col + 2 * (3 - 2 * z)}
    at_xa = {"row": row + 2 * (1 - 2 * lax.rem(x, 2)), "col": col}
    at_xb = {"row": row + 2 * (3 - 2 * x), "col": col}
    at_yh = {"row": row + 1 - 2 * yh, "col": col}
    bits = (yl, za, zb)
    partner = (at_y, at_za, at_zb)

    count = [0]
    sent = []

    def push(src, dst, where):
        k = count[0]
        count[0] += 1
        copy = pltpu.make_async_remote_copy(
            src_ref=src, dst_ref=dst, send_sem=send_sem.at[k], recv_sem=recv_sem.at[k],
            device_id=where, device_id_type=pl.DeviceIdType.MESH,
        )
        copy.start()
        sent.append(copy)
        return copy

    lcount = [0]

    def local(src, dst):
        k = lcount[0]
        lcount[0] += 1
        copy = pltpu.make_async_copy(src, dst, local_sem.at[k])
        copy.start()
        return copy

    def cols(h):
        return pl.ds(pl.multiple_of(h * 2048, 2048), 2048)

    barrier = pltpu.get_barrier_semaphore()
    for where in (at_core, at_y, at_za, at_zb, at_xa, at_xb, at_yh):
        pl.semaphore_signal(barrier, inc=1, device_id=where, device_id_type=pl.DeviceIdType.MESH)

    tok_in = local(tok, TA.at[core, xb, xa, yh])
    cot_in = local(cot, CA.at[core, xb, xa, yh])
    si_far = local(win.at[:, cols(other)], DI.at[:, cols(other)])
    si_own = local(win.at[:, cols(core)], DI.at[:, cols(core)])
    so_far = local(wout.at[cols(other)], DO.at[cols(other)])
    so_own = local(wout.at[cols(core)], DO.at[cols(core)])

    def spread(scalar):
        return jnp.full((16, BLOCK), scalar.astype(F32), F32).astype(BF)

    def expand_in(h, dst):
        def step(j, carry):
            for i in range(4):
                dst[i, :, pl.ds(pl.multiple_of(j * BLOCK, BLOCK), BLOCK)] = spread(
                    mask_in[i, h * 16 + j]
                )
            return carry
        lax.fori_loop(0, 16, step, 0)

    def expand_out(h, dst):
        def step(i, carry):
            for j in range(4):
                dst[i, :, BLOCK * j : BLOCK * (j + 1)] = spread(mask_out_t[j, h * 16 + i])
            return carry
        lax.fori_loop(0, 16, step, 0)

    expand_in(other, MIS)
    expand_in(core, MI.at[core])
    expand_out(other, MOS)
    expand_out(core, MO.at[core])
    pl.semaphore_wait(barrier, 7)

    def gather_y(A):
        return {"y": push(A.at[core, xb, xa, yh], A.at[core, xb, xa, yh], at_yh)}

    def gather_first(A, c):
        c["a0"] = push(A.at[core, xb, xa, yh, 0], A.at[core, xb, xa, yh, 0], at_xb)
        c["b0"] = push(A.at[core, xb, xa, yh, 1], A.at[core, xb, xa, yh, 1], at_xa)

    def gather_second(A, c, v, tag):
        c["a" + tag].wait_recv()
        c["A" + tag] = push(A.at[core, :, xa, v, 0], A.at[core, :, xa, v, 0], at_xa)
        c["b" + tag].wait_recv()
        c["B" + tag] = push(A.at[core, xb, :, v, 1], A.at[core, xb, :, v, 1], at_xb)

    def gather_third(A, c, v):
        c["y"].wait_recv()
        c["a1"] = push(A.at[core, xb, xa, v, 0], A.at[core, xb, xa, v, 0], at_xb)
        c["b1"] = push(A.at[core, xb, xa, v, 1], A.at[core, xb, xa, v, 1], at_xa)

    def gather_cross(A, c, v, tag):
        c["A" + tag].wait_recv()
        c["B" + tag].wait_recv()
        c["c" + tag] = push(A.at[core, :, :, v], A.at[core, :, :, v], at_core)

    def mask_in_half(h, m, dst):
        def step(i, carry):
            r = pl.multiple_of(i * BLOCK, BLOCK)
            w = DI[pl.ds(r, BLOCK), cols(h)].reshape(8, 16, 2048)
            dst[pl.ds(r, BLOCK), :] = (w * m[i][None]).reshape(BLOCK, 2048)
            return carry
        lax.fori_loop(0, 4, step, 0)

    def mask_out_half(h, m, dst):
        def step(i, carry):
            r = pl.multiple_of(i * BLOCK, BLOCK)
            w = DO[pl.ds(pl.multiple_of(h * 2048 + r, BLOCK), BLOCK), :].reshape(8, 16, 512)
            dst[pl.ds(r, BLOCK), :] = (w * m[i][None]).reshape(BLOCK, 512)
            return carry
        lax.fori_loop(0, 16, step, 0)

    tok_in.wait()
    tc = gather_y(TA)
    gather_first(TA, tc)
    cot_in.wait()
    cc = gather_y(CA)
    si_far.wait()
    mask_in_half(other, MIS, FI)
    wi_c = push(FI, WI.at[core], at_core)
    gather_second(TA, tc, yh, "0")
    gather_first(CA, cc)
    si_own.wait()
    mask_in_half(core, MI.at[core], WI.at[core])
    so_far.wait()
    mask_out_half(other, MOS, FO)
    gather_cross(TA, tc, yh, "0")
    wo_c = push(FO, WO.at[core], at_core)
    gather_third(TA, tc, 1 - yh)
    wi_c.wait_recv()
    tc["c0"].wait_recv()

    def part_rows(j, half, v):
        out = None
        for k in range(2):
            t = dot(TA[k, half, :, v].reshape(192, 512), WI[k, :, WIDE * j : WIDE * (j + 1)], 1, 0)
            out = t if out is None else out + t
        return out.reshape(2, 96, WIDE)

    def part_in(j, half):
        out = None
        for k in range(2):
            t = dot(TA[k, half].reshape(384, 512), WI[k, :, WIDE * j : WIDE * (j + 1)], 1, 0)
            out = t if out is None else out + t
        return out.reshape(2, 2, 96, WIDE)

    def part_out(j, half):
        out = None
        for k in range(2):
            t = dot(CA[k, half].reshape(384, 512), WO[k, WIDE * j : WIDE * (j + 1), :], 1, 1)
            out = t if out is None else out + t
        return out.reshape(2, 2, 96, WIDE)

    streams = ((part_in, S1a, R1a, ACa, S2a, R2a, S3a, R3a), (part_out, S1b, R1b, ACb, S2b, R2b, S3b, R3b))
    first = [[None] * CHUNKS for _ in range(2)]
    second = [[None] * CHUNKS for _ in range(2)]
    third = [[None] * CHUNKS for _ in range(2)]

    def halve_rows(j, v):
        d = ORDERS[j][0]
        S1a[j, :, v] = part_rows(j, 1 - bits[d], v).astype(BF)
        c = push(S1a.at[j, :, v], R1a.at[j, :, v], partner[d])
        first[0][j] = (first[0][j] or ()) + (c,)

    def halve_first(s, j):
        part, S1, R1, AC, S2, R2, S3, R3 = streams[s]
        d = ORDERS[j][0]
        S1[j] = part(j, 1 - bits[d]).astype(BF)
        first[s][j] = (push(S1.at[j], R1.at[j], partner[d]),)

    def halve_kept(s, j):
        part, S1, R1, AC, S2, R2, S3, R3 = streams[s]
        AC[j] = part(j, bits[ORDERS[j][0]])

    def halve_second(s, j):
        part, S1, R1, AC, S2, R2, S3, R3 = streams[s]
        d = ORDERS[j][1]
        away, keep = 1 - bits[d], bits[d]
        for c in first[s][j]:
            c.wait_recv()
        S2[j] = (AC[j, away] + R1[j, away].astype(F32)).astype(BF)
        second[s][j] = push(S2.at[j], R2.at[j], partner[d])
        AC[j, keep] = AC[j, keep] + R1[j, keep].astype(F32)

    def halve_third(s, j):
        part, S1, R1, AC, S2, R2, S3, R3 = streams[s]
        base, d = bits[ORDERS[j][1]], ORDERS[j][2]
        away, keep = 1 - bits[d], bits[d]
        second[s][j].wait_recv()
        S3[j] = (AC[j, base, away] + R2[j, away].astype(F32)).astype(BF)
        third[s][j] = push(S3.at[j], R3.at[j], partner[d])
        AC[j, base, keep] = AC[j, base, keep] + R2[j, keep].astype(F32)

    def whole(s, j):
        part, S1, R1, AC, S2, R2, S3, R3 = streams[s]
        third[s][j].wait_recv()
        base, last = bits[ORDERS[j][1]], bits[ORDERS[j][2]]
        return AC[j, base, last] + R3[j].astype(F32), base, last

    d1 = [[None] * CHUNKS for _ in range(2)]
    d2 = [[None] * CHUNKS for _ in range(2)]
    d3 = [[None] * CHUNKS for _ in range(2)]

    def double_first(s, j, A):
        m = [bits[d] for d in ORDERS[j]]
        at = A.at[j, 4 * m[0] + 2 * m[1] + m[2]]
        d1[s][j] = push(at, at, partner[ORDERS[j][2]])

    def double_second(s, j, A):
        m = [bits[d] for d in ORDERS[j]]
        d1[s][j].wait_recv()
        at = A.at[j, pl.ds(4 * m[0] + 2 * m[1], 2)]
        d2[s][j] = push(at, at, partner[ORDERS[j][1]])

    def double_third(s, j, A):
        m = [bits[d] for d in ORDERS[j]]
        d2[s][j].wait_recv()
        at = A.at[j, pl.ds(4 * m[0], 4)]
        d3[s][j] = push(at, at, partner[ORDERS[j][0]])

    def make_hidden(j):
        m = [bits[d] for d in ORDERS[j]]
        v, base, last = whole(0, j)
        value, slope = gelu_both(v)
        H[j, 4 * m[0] + 2 * m[1] + m[2]] = value.astype(BF)
        ACa[j, base, last] = slope
        double_first(0, j, H)

    def make_grad(j):
        m = [bits[d] for d in ORDERS[j]]
        v, base, last = whole(1, j)
        G[j, 4 * m[0] + 2 * m[1] + m[2]] = (v * ACa[j, base, last]).astype(BF)
        double_first(1, j, G)

    each = range(CHUNKS)
    for j in range(4):
        halve_rows(j, yh)
    gather_second(TA, tc, 1 - yh, "1")
    for j in range(4, 8):
        halve_rows(j, yh)
    gather_second(CA, cc, yh, "0")
    gather_third(CA, cc, 1 - yh)
    gather_cross(TA, tc, 1 - yh, "1")
    so_own.wait()
    mask_out_half(core, MO.at[core], WO.at[core])
    tc["c1"].wait_recv()
    for j in range(4):
        halve_rows(j, 1 - yh)
    gather_second(CA, cc, 1 - yh, "1")
    gather_cross(CA, cc, yh, "0")
    for j in range(4, 8):
        halve_rows(j, 1 - yh)
    for j in range(4):
        halve_kept(0, j)
    gather_cross(CA, cc, 1 - yh, "1")
    mi_c = push(MIS, MI.at[core], at_core)
    mo_c = push(MOS, MO.at[core], at_core)
    for j in range(4, 8):
        halve_kept(0, j)
    wo_c.wait_recv()
    cc["c0"].wait_recv()
    cc["c1"].wait_recv()
    for j in each:
        halve_first(1, j)
    for j in each:
        halve_second(0, j)
    for j in each:
        halve_kept(1, j)
    for j in each:
        halve_third(0, j)
    for j in each:
        halve_second(1, j)
    for j in each:
        make_hidden(j)
    for j in each:
        halve_third(1, j)
    for j in each:
        double_second(0, j, H)
    for j in each:
        make_grad(j)
    for j in each:
        double_third(0, j, H)
    for j in each:
        double_second(1, j, G)

    every = slice(None)

    def lanes(u):
        return slice(256 * u, 256 * (u + 1))

    def out_part(A, lo, hi, u, k, weight, right_dim):
        def step(h, carry):
            left = jnp.concatenate(
                [A[i, pl.ds(4 * h, 4)].reshape(384, WIDE) for i in range(lo, hi)], axis=1
            )
            got = dot(left, weight(lo, hi, u, k), 1, right_dim).reshape(2, 2, 2, 48, 256)
            if lo == 0:
                R[k, u, h] = got
            else:
                R[k, u, h] = R[k, u, h] + got
            return carry
        lax.fori_loop(0, 2, step, 0)

    def wout_of(lo, hi, u, k):
        return WO[k, WIDE * lo : WIDE * hi, lanes(u)]

    def win_of(lo, hi, u, k):
        return WI[k, lanes(u), WIDE * lo : WIDE * hi]

    def row_cross(n, u):
        return push(R.at[other, u], RX.at[n, u], at_core)

    def full(n, u, idx):
        return R[(core, u) + idx] + RX[(n, u) + idx]

    def row_first(cross, n, u):
        cross.wait_recv()
        T1[n, u, 0] = full(n, u, (1 - xb, every, every, 0)).astype(BF)
        a = push(T1.at[n, u, 0], U1.at[n, u, 0], at_xb)
        T1[n, u, 1] = full(n, u, (every, 1 - xa, every, 1)).astype(BF)
        b = push(T1.at[n, u, 1], U1.at[n, u, 1], at_xa)
        return a, b

    def row_second(copies, n, u):
        copies[0].wait_recv()
        T2[n, u, 0] = (full(n, u, (xb, 1 - xa, every, 0)) + U1[n, u, 0, 1 - xa].astype(F32)).astype(BF)
        a = push(T2.at[n, u, 0], U2.at[n, u, 0], at_xa)
        copies[1].wait_recv()
        T2[n, u, 1] = (full(n, u, (1 - xb, xa, every, 1)) + U1[n, u, 1, 1 - xb].astype(F32)).astype(BF)
        b = push(T2.at[n, u, 1], U2.at[n, u, 1], at_xb)
        return a, b

    def row_third(copies, n, u):
        def row_sum(v, hf):
            near = (xa, xb)[hf]
            return (
                full(n, u, (xb, xa, v, hf))
                + U1[n, u, hf, near, v].astype(F32)
                + U2[n, u, hf, v].astype(F32)
            )

        for hf in range(2):
            copies[hf].wait_recv()
            T3[n, u, hf] = row_sum(1 - yh, hf).astype(BF)
        c = push(T3.at[n, u], U3.at[n, u], at_yh)
        for hf in range(2):
            KEEP[n, u, hf] = row_sum(yh, hf)
        return c

    def row_last(copy, n, u, out):
        copy.wait_recv()
        out[:, :, lanes(u)] = (KEEP[n, u] + U3[n, u].astype(F32)).astype(BF)

    def out_grad(lo, hi, k, to):
        def step(j, carry):
            left = H[j].reshape(768, WIDE)
            got = dot(left, CA[k].reshape(768, 512), 0, 0).reshape(2, 8, 16, 512)
            m = MO[k, pl.ds(2 * j, 2)].astype(F32)
            to(j, (got * m[:, None]).reshape(WIDE, 512).astype(BF))
            return carry
        lax.fori_loop(lo, hi, step, 0)

    def far_out(j, v):
        FO[pl.ds(pl.multiple_of(j * WIDE, WIDE), WIDE), :] = v

    def own_out(j, v):
        DO[pl.ds(pl.multiple_of(core * 2048 + j * WIDE, WIDE), WIDE), :] = v

    def in_grad(lo, hi, k, to):
        def step(i, carry):
            d = pl.multiple_of(i * WIDE, WIDE)
            left = TA[k, :, :, :, :, :, pl.ds(d, WIDE)].reshape(768, WIDE)
            for j in range(CHUNKS):
                got = dot(left, G[j].reshape(768, WIDE), 0, 0).reshape(2, 8, 16, WIDE)
                m = MI[k, pl.ds(2 * i, 2), :, WIDE * j : WIDE * (j + 1)].astype(F32)
                to(d, j, (got * m[:, None]).reshape(WIDE, WIDE).astype(BF))
            return carry
        lax.fori_loop(lo, hi, step, 0)

    def far_in(d, j, v):
        FI[pl.ds(d, WIDE), WIDE * j : WIDE * (j + 1)] = v

    def own_in(d, j, v):
        DI[pl.ds(d, WIDE), pl.ds(pl.multiple_of(core * 2048 + WIDE * j, WIDE), WIDE)] = v

    both = range(2)
    for j in range(4):
        d3[0][j].wait_recv()
    for k in both:
        for u in both:
            out_part(H, 0, 4, u, k, wout_of, 0)
    for j in range(4, 8):
        d3[0][j].wait_recv()
    cross0 = []
    for u in both:
        out_part(H, 4, 8, u, other, wout_of, 0)
        cross0.append(row_cross(0, u))
    for j in range(4):
        double_third(1, j, G)
    for u in both:
        out_part(H, 4, 8, u, core, wout_of, 0)
    for j in range(4, 8):
        double_third(1, j, G)
    pair = [row_first(cross0[u], 0, u) for u in both]
    wo_c.wait_send()
    mo_c.wait_recv()
    out_grad(0, 4, other, far_out)
    pair = [row_second(pair[u], 0, u) for u in both]
    out_grad(4, 8, other, far_out)
    dwo_far = push(FO, DO.at[cols(core)], at_core)
    last0 = [row_third(pair[u], 0, u) for u in both]
    for c in cross0:
        c.wait_send()
    for j in range(4):
        d3[1][j].wait_recv()
    for k in both:
        for u in both:
            out_part(G, 0, 4, u, k, win_of, 1)
    for j in range(4, 8):
        d3[1][j].wait_recv()
    cross1 = []
    for u in both:
        out_part(G, 4, 8, u, other, win_of, 1)
        cross1.append(row_cross(1, u))
    for u in both:
        out_part(G, 4, 8, u, core, win_of, 1)
    pair = [row_first(cross1[u], 1, u) for u in both]
    wi_c.wait_send()
    mi_c.wait_recv()
    in_grad(0, 2, other, far_in)
    dwi_far = push(FI, DI.at[:, cols(core)], at_core)
    pair = [row_second(pair[u], 1, u) for u in both]
    in_grad(0, 1, core, own_in)
    last1 = [row_third(pair[u], 1, u) for u in both]
    in_grad(1, 2, core, own_in)
    out_grad(0, 8, core, own_out)
    for u in both:
        row_last(last0[u], 0, u, res_o)
    for u in both:
        row_last(last1[u], 1, u, tg_o)
    dwo_far.wait_recv()
    dwi_far.wait_recv()
    waited = [wo_c, wi_c] + cross0
    for c in sent:
        if not any(c is w for w in waited):
            c.wait_send()


def body(tokens, weight_in, mask_in, weight_out, mask_out, cotangent):
    anywhere = pl.BlockSpec(memory_space=pl.ANY)
    vmem = pl.BlockSpec(memory_space=pltpu.VMEM)
    smem = pl.BlockSpec(memory_space=pltpu.SMEM)

    def halving():
        return [
            pltpu.VMEM((CHUNKS, 2, 2, 96, WIDE), BF),
            pltpu.VMEM((CHUNKS, 2, 2, 96, WIDE), BF),
            pltpu.VMEM((CHUNKS, 2, 2, 96, WIDE), F32),
            pltpu.VMEM((CHUNKS, 2, 96, WIDE), BF),
            pltpu.VMEM((CHUNKS, 2, 96, WIDE), BF),
            pltpu.VMEM((CHUNKS, 96, WIDE), BF),
            pltpu.VMEM((CHUNKS, 96, WIDE), BF),
        ]

    result, tokens_grad, dwi, dwo = pl.pallas_call(
        kernel,
        out_shape=(
            OUT_KIND((2, 48, 512), BF),
            OUT_KIND((2, 48, 512), BF),
            OUT_KIND((512, 4096), BF),
            OUT_KIND((4096, 512), BF),
        ),
        in_specs=[anywhere] * 4 + [smem] * 2,
        out_specs=(vmem,) * 4,
        scratch_shapes=[
            pltpu.VMEM((2, 2, 2, 2, 2, 48, 512), BF),
            pltpu.VMEM((2, 2, 2, 2, 2, 48, 512), BF),
            pltpu.VMEM((2, 512, 2048), BF),
            pltpu.VMEM((2, 2048, 512), BF),
            pltpu.VMEM((512, 2048), BF),
            pltpu.VMEM((2048, 512), BF),
            pltpu.VMEM((4, 16, 2048), BF),
            pltpu.VMEM((2, 4, 16, 2048), BF),
            pltpu.VMEM((16, 16, 512), BF),
            pltpu.VMEM((2, 16, 16, 512), BF),
        ]
        + halving()
        + halving()
        + [
            pltpu.VMEM((CHUNKS, 8, 96, WIDE), BF),
            pltpu.VMEM((CHUNKS, 8, 96, WIDE), BF),
            pltpu.VMEM((2, 2, 2, 2, 2, 2, 48, 256), F32),
            pltpu.VMEM((2, 2, 2, 2, 2, 2, 48, 256), F32),
            pltpu.VMEM((2, 2, 2, 2, 2, 48, 256), BF),
            pltpu.VMEM((2, 2, 2, 2, 2, 48, 256), BF),
            pltpu.VMEM((2, 2, 2, 2, 48, 256), BF),
            pltpu.VMEM((2, 2, 2, 2, 48, 256), BF),
            pltpu.VMEM((2, 2, 2, 48, 256), BF),
            pltpu.VMEM((2, 2, 2, 48, 256), BF),
            pltpu.VMEM((2, 2, 2, 48, 256), F32),
            pltpu.SemaphoreType.DMA((N_COPIES,)),
            pltpu.SemaphoreType.DMA((N_COPIES,)),
            pltpu.SemaphoreType.DMA((8,)),
        ],
        compiler_params=pltpu.CompilerParams(
            collective_id=0, has_side_effects=True, vmem_limit_bytes=VMEM_BYTES
        ),
    )(tokens.reshape(2, 48, 512), cotangent.reshape(2, 48, 512), weight_in, weight_out, mask_in, mask_out.T)
    return result.reshape(96, 512), tokens_grad.reshape(96, 512), dwi, dwo


def solution(mesh):
    return jax.shard_map(
        body,
        mesh=mesh,
        in_specs=(
            P("row", "col"),
            P("col", "row"),
            P("col", "row"),
            P("row", "col"),
            P("row", "col"),
            P("row", "col"),
        ),
        out_specs=(P("row", "col"), P("row", "col"), P("col", "row"), P("row", "col")),
        check_vma=False,
    )
```

```python
import jax
import jax.numpy as jnp
from jax import lax
from jax.experimental import pallas as pl
from jax.experimental.pallas import tpu as pltpu
from jax.sharding import PartitionSpec as P

BLOCK = 128
CHUNKS = 4
WIDE = 512
BF = jnp.bfloat16
F32 = jnp.float32

root_two_pi = 0.7978845608
cubic_coef = 0.044715

ORDERS = ((0, 1, 2), (1, 2, 0), (2, 0, 1))
PARTS = 3


def dot(left, right, left_dim, right_dim):
    return lax.dot_general(
        left, right, (((left_dim,), (right_dim,)), ((), ())), preferred_element_type=F32
    )


def gelu_both(values):
    tangent = jnp.tanh(root_two_pi * (values + cubic_coef * values * values * values))
    value = 0.5 * values * (1.0 + tangent)
    slope = 0.5 * (1.0 + tangent) + 0.5 * values * (1.0 - tangent * tangent) * root_two_pi * (
        1.0 + 3.0 * cubic_coef * values * values
    )
    return value, slope
OUT_KIND = pltpu.VMEM
VMEM_BYTES = 53 * 1024 * 1024


N_COPIES = 256


def kernel(
    tok, cot, win, wout, mask_in, mask_out_t,
    res_o, tg_o, DI, DO,
    TA, CA, WI, WO, FI, FO, MIS, MI, MOS, MO,
    S1a, R1a, ACa, S2a, R2a, S3a, R3a,
    S1b, R1b, ACb, S2b, R2b, S3b, R3b,
    H, G, R, RX, T1, U1, T2, U2, T3, U3, KEEP,
    send_sem, recv_sem, local_sem,
):
    row = lax.axis_index("row")
    col = lax.axis_index("col")
    x, yh = lax.div(row, 2), lax.rem(row, 2)
    yl = lax.div(col, 8)
    z = lax.div(lax.rem(col, 8), 2)
    core = lax.rem(col, 2)
    other = 1 - core
    xb, xa = lax.div(x, 2), lax.rem(lax.div(x + 1, 2), 2)
    zb, za = lax.div(z, 2), lax.rem(lax.div(z + 1, 2), 2)
    at_core = {"row": row, "col": col + 1 - 2 * core}
    at_y = {"row": row, "col": col + 8 - 16 * yl}
    at_za = {"row": row, "col": col + 2 * (1 - 2 * lax.rem(z, 2))}
    at_zb = {"row": row, "col": col + 2 * (3 - 2 * z)}
    at_xa = {"row": row + 2 * (1 - 2 * lax.rem(x, 2)), "col": col}
    at_xb = {"row": row + 2 * (3 - 2 * x), "col": col}
    at_yh = {"row": row + 1 - 2 * yh, "col": col}
    bits = (yl, za, zb)
    partner = (at_y, at_za, at_zb)

    count = [0]
    sent = []

    def push(src, dst, where):
        k = count[0]
        count[0] += 1
        copy = pltpu.make_async_remote_copy(
            src_ref=src, dst_ref=dst, send_sem=send_sem.at[k], recv_sem=recv_sem.at[k],
            device_id=where, device_id_type=pl.DeviceIdType.MESH,
        )
        copy.start()
        sent.append(copy)
        return copy

    lcount = [0]

    def local(src, dst):
        k = lcount[0]
        lcount[0] += 1
        copy = pltpu.make_async_copy(src, dst, local_sem.at[k])
        copy.start()
        return copy

    def cols(h):
        return pl.ds(pl.multiple_of(h * 2048, 2048), 2048)

    barrier = pltpu.get_barrier_semaphore()
    for where in (at_core, at_y, at_za, at_zb, at_xa, at_xb, at_yh):
        pl.semaphore_signal(barrier, inc=1, device_id=where, device_id_type=pl.DeviceIdType.MESH)

    tok_in = local(tok, TA.at[core, xb, xa, yh])
    cot_in = local(cot, CA.at[core, xb, xa, yh])
    si_far = local(win.at[:, cols(other)], DI.at[:, cols(other)])
    si_own = local(win.at[:, cols(core)], DI.at[:, cols(core)])
    so_far = local(wout.at[cols(other)], DO.at[cols(other)])
    so_own = local(wout.at[cols(core)], DO.at[cols(core)])

    def spread(scalar):
        return jnp.full((16, BLOCK), scalar.astype(F32), F32).astype(BF)

    def expand_in(h, dst):
        def step(j, carry):
            for i in range(4):
                dst[i, :, pl.ds(pl.multiple_of(j * BLOCK, BLOCK), BLOCK)] = spread(
                    mask_in[i, h * 16 + j]
                )
            return carry
        lax.fori_loop(0, 16, step, 0)

    def expand_out(h, dst):
        def step(i, carry):
            for j in range(4):
                dst[i, :, BLOCK * j : BLOCK * (j + 1)] = spread(mask_out_t[j, h * 16 + i])
            return carry
        lax.fori_loop(0, 16, step, 0)

    expand_in(other, MIS)
    expand_in(core, MI.at[core])
    expand_out(other, MOS)
    expand_out(core, MO.at[core])
    pl.semaphore_wait(barrier, 7)

    def gather_y(A, c):
        for hf in range(2):
            at = A.at[core, xb, xa, yh, hf]
            c["y%d" % hf] = push(at, at, at_yh)

    def gather_first(A, c):
        c["a0"] = push(A.at[core, xb, xa, yh, 0], A.at[core, xb, xa, yh, 0], at_xb)
        c["b0"] = push(A.at[core, xb, xa, yh, 1], A.at[core, xb, xa, yh, 1], at_xa)

    def gather_second(A, c, v, tag):
        c["a" + tag].wait_recv()
        c["A" + tag] = push(A.at[core, :, xa, v, 0], A.at[core, :, xa, v, 0], at_xa)
        c["b" + tag].wait_recv()
        c["B" + tag] = push(A.at[core, xb, :, v, 1], A.at[core, xb, :, v, 1], at_xb)

    def gather_third(A, c, v):
        c["y0"].wait_recv()
        c["a1"] = push(A.at[core, xb, xa, v, 0], A.at[core, xb, xa, v, 0], at_xb)
        c["y1"].wait_recv()
        c["b1"] = push(A.at[core, xb, xa, v, 1], A.at[core, xb, xa, v, 1], at_xa)

    def gather_cross(A, c, v, tag):
        c["A" + tag].wait_recv()
        one = push(A.at[core, :, :, v, 0], A.at[core, :, :, v, 0], at_core)
        c["B" + tag].wait_recv()
        two = push(A.at[core, :, :, v, 1], A.at[core, :, :, v, 1], at_core)
        c["c" + tag] = (one, two)

    def crossed(c, tag):
        for copy in c["c" + tag]:
            copy.wait_recv()

    def mask_in_half(h, m, dst):
        def step(i, carry):
            r = pl.multiple_of(i * BLOCK, BLOCK)
            w = DI[pl.ds(r, BLOCK), cols(h)].reshape(8, 16, 2048)
            dst[pl.ds(r, BLOCK), :] = (w * m[i][None]).reshape(BLOCK, 2048)
            return carry
        lax.fori_loop(0, 4, step, 0)

    def mask_out_half(h, m, dst):
        def step(i, carry):
            r = pl.multiple_of(i * BLOCK, BLOCK)
            w = DO[pl.ds(pl.multiple_of(h * 2048 + r, BLOCK), BLOCK), :].reshape(8, 16, 512)
            dst[pl.ds(r, BLOCK), :] = (w * m[i][None]).reshape(BLOCK, 512)
            return carry
        lax.fori_loop(0, 16, step, 0)

    tok_in.wait()
    tc, cc = {}, {}
    gather_y(TA, tc)
    gather_first(TA, tc)
    si_far.wait()
    mask_in_half(other, MIS, FI)
    wi_c = push(FI, WI.at[core], at_core)
    gather_second(TA, tc, yh, "0")
    cot_in.wait()
    gather_first(CA, cc)
    si_own.wait()
    mask_in_half(core, MI.at[core], WI.at[core])
    gather_third(TA, tc, 1 - yh)
    gather_y(CA, cc)
    gather_cross(TA, tc, yh, "0")
    so_far.wait()
    mask_out_half(other, MOS, FO)
    wo_c = push(FO, WO.at[core], at_core)
    wi_c.wait_recv()
    crossed(tc, "0")

    def part_in(j, v):
        out = None
        for k in range(2):
            t = dot(TA[k, :, :, v].reshape(384, 512), WI[k, :, WIDE * j : WIDE * (j + 1)], 1, 0)
            out = t if out is None else out + t
        return out.reshape(2, 2, PARTS, 32, WIDE)

    def part_out(j, v):
        out = None
        for k in range(2):
            t = dot(CA[k, :, :, v].reshape(384, 512), WO[k, WIDE * j : WIDE * (j + 1), :], 1, 1)
            out = t if out is None else out + t
        return out.reshape(2, 2, PARTS, 32, WIDE)

    streams = ((part_in, S1a, R1a, ACa, S2a, R2a, S3a, R3a), (part_out, S1b, R1b, ACb, S2b, R2b, S3b, R3b))
    units = [(j, p) for j in range(CHUNKS) for p in range(PARTS)]
    first = [{u: () for u in units} for _ in range(2)]
    second, third = [{}, {}], [{}, {}]

    def halve_first(s, j, v):
        part, S1, R1, AC, S2, R2, S3, R3 = streams[s]
        got = part(j, v)
        for p in range(PARTS):
            d = ORDERS[p][0]
            low = bits[d] == 0
            S1[j, p, :, v] = jnp.where(low, got[1, :, p], got[0, :, p]).astype(BF)
            c = push(S1.at[j, p, :, v], R1.at[j, p, :, v], partner[d])
            first[s][j, p] += (c,)
        for p in range(PARTS):
            low = bits[ORDERS[p][0]] == 0
            AC[j, p, :, v] = jnp.where(low, got[0, :, p], got[1, :, p])

    def halve_second(s, j, p):
        part, S1, R1, AC, S2, R2, S3, R3 = streams[s]
        d = ORDERS[p][1]
        away, keep = 1 - bits[d], bits[d]
        for c in first[s][j, p]:
            c.wait_recv()
        S2[j, p] = (AC[j, p, away] + R1[j, p, away].astype(F32)).astype(BF)
        second[s][j, p] = push(S2.at[j, p], R2.at[j, p], partner[d])
        AC[j, p, keep] = AC[j, p, keep] + R1[j, p, keep].astype(F32)

    def halve_third(s, j, p):
        part, S1, R1, AC, S2, R2, S3, R3 = streams[s]
        base, d = bits[ORDERS[p][1]], ORDERS[p][2]
        away, keep = 1 - bits[d], bits[d]
        second[s][j, p].wait_recv()
        S3[j, p] = (AC[j, p, base, away] + R2[j, p, away].astype(F32)).astype(BF)
        third[s][j, p] = push(S3.at[j, p], R3.at[j, p], partner[d])
        AC[j, p, base, keep] = AC[j, p, base, keep] + R2[j, p, keep].astype(F32)

    def whole(s, j, p):
        part, S1, R1, AC, S2, R2, S3, R3 = streams[s]
        third[s][j, p].wait_recv()
        base, last = bits[ORDERS[p][1]], bits[ORDERS[p][2]]
        return AC[j, p, base, last] + R3[j, p].astype(F32), base, last

    d1, d2, d3 = [{}, {}], [{}, {}], [{}, {}]

    def double_first(s, j, p, A):
        m = [bits[d] for d in ORDERS[p]]
        at = A.at[j, 4 * m[0] + 2 * m[1] + m[2], p]
        d1[s][j, p] = push(at, at, partner[ORDERS[p][2]])

    def double_second(s, j, p, A):
        m = [bits[d] for d in ORDERS[p]]
        d1[s][j, p].wait_recv()
        at = A.at[j, pl.ds(4 * m[0] + 2 * m[1], 2), p]
        d2[s][j, p] = push(at, at, partner[ORDERS[p][1]])

    def double_third(s, j, p, A):
        m = [bits[d] for d in ORDERS[p]]
        d2[s][j, p].wait_recv()
        at = A.at[j, pl.ds(4 * m[0], 4), p]
        d3[s][j, p] = push(at, at, partner[ORDERS[p][0]])

    def make_hidden(j, p):
        m = [bits[d] for d in ORDERS[p]]
        v, base, last = whole(0, j, p)
        value, slope = gelu_both(v)
        H[j, 4 * m[0] + 2 * m[1] + m[2], p] = value.astype(BF)
        ACa[j, p, base, last] = slope
        double_first(0, j, p, H)

    def make_grad(j, p):
        m = [bits[d] for d in ORDERS[p]]
        v, base, last = whole(1, j, p)
        G[j, 4 * m[0] + 2 * m[1] + m[2], p] = (v * ACa[j, p, base, last]).astype(BF)
        double_first(1, j, p, G)

    far = 1 - yh
    halve_first(0, 0, yh)
    gather_second(TA, tc, far, "1")
    halve_first(0, 1, yh)
    gather_second(CA, cc, yh, "0")
    halve_first(0, 2, yh)
    gather_cross(TA, tc, far, "1")
    halve_first(0, 3, yh)
    so_own.wait()
    mask_out_half(core, MO.at[core], WO.at[core])
    gather_third(CA, cc, far)
    gather_cross(CA, cc, yh, "0")
    crossed(tc, "1")
    halve_first(0, 0, far)
    halve_first(0, 1, far)
    gather_second(CA, cc, far, "1")
    halve_first(0, 2, far)
    halve_first(0, 3, far)
    wo_c.wait_recv()
    crossed(cc, "0")
    halve_first(1, 0, yh)
    halve_first(1, 1, yh)
    gather_cross(CA, cc, far, "1")
    mi_c = push(MIS, MI.at[core], at_core)
    mo_c = push(MOS, MO.at[core], at_core)
    halve_first(1, 2, yh)
    halve_first(1, 3, yh)
    crossed(cc, "1")
    for j in range(CHUNKS):
        halve_first(1, j, far)
    for u in units:
        halve_second(0, *u)
    for u in units:
        halve_third(0, *u)
    for u in units:
        halve_second(1, *u)
    for u in units:
        make_hidden(*u)
    for u in units:
        halve_third(1, *u)
    for u in units:
        double_second(0, *u, H)
    for u in units:
        make_grad(*u)
    for u in units:
        double_third(0, *u, H)
    for u in units:
        double_second(1, *u, G)

    every = slice(None)

    def lanes(u):
        return slice(256 * u, 256 * (u + 1))

    def out_part(A, lo, hi, u, k, weight, right_dim):
        def step(h, carry):
            left = jnp.concatenate(
                [A[i, pl.ds(4 * h, 4)].reshape(384, WIDE) for i in range(lo, hi)], axis=1
            )
            got = dot(left, weight(lo, hi, u, k), 1, right_dim).reshape(2, 2, 2, 48, 256)
            if lo == 0:
                R[k, u, h] = got
            else:
                R[k, u, h] = R[k, u, h] + got
            return carry
        lax.fori_loop(0, 2, step, 0)

    def wout_of(lo, hi, u, k):
        return WO[k, WIDE * lo : WIDE * hi, lanes(u)]

    def win_of(lo, hi, u, k):
        return WI[k, lanes(u), WIDE * lo : WIDE * hi]

    def row_cross(n, u):
        return push(R.at[other, u], RX.at[n, u], at_core)

    def full(n, u, idx):
        return R[(core, u) + idx] + RX[(n, u) + idx]

    def row_first(cross, n, u):
        cross.wait_recv()
        T1[n, u, 0] = full(n, u, (1 - xb, every, every, 0)).astype(BF)
        a = push(T1.at[n, u, 0], U1.at[n, u, 0], at_xb)
        T1[n, u, 1] = full(n, u, (every, 1 - xa, every, 1)).astype(BF)
        b = push(T1.at[n, u, 1], U1.at[n, u, 1], at_xa)
        return a, b

    def row_second(copies, n, u):
        copies[0].wait_recv()
        T2[n, u, 0] = (full(n, u, (xb, 1 - xa, every, 0)) + U1[n, u, 0, 1 - xa].astype(F32)).astype(BF)
        a = push(T2.at[n, u, 0], U2.at[n, u, 0], at_xa)
        copies[1].wait_recv()
        T2[n, u, 1] = (full(n, u, (1 - xb, xa, every, 1)) + U1[n, u, 1, 1 - xb].astype(F32)).astype(BF)
        b = push(T2.at[n, u, 1], U2.at[n, u, 1], at_xb)
        return a, b

    def row_third(copies, n, u):
        def row_sum(v, hf):
            near = (xa, xb)[hf]
            return (
                full(n, u, (xb, xa, v, hf))
                + U1[n, u, hf, near, v].astype(F32)
                + U2[n, u, hf, v].astype(F32)
            )

        for hf in range(2):
            copies[hf].wait_recv()
            T3[n, u, hf] = row_sum(1 - yh, hf).astype(BF)
            KEEP[n, u, hf] = row_sum(yh, hf)

    def row_fourth(n, u):
        return push(T3.at[n, u], U3.at[n, u], at_yh)

    def row_last(copy, n, u, out):
        copy.wait_recv()
        out[:, :, lanes(u)] = (KEEP[n, u] + U3[n, u].astype(F32)).astype(BF)

    def out_grad(k, to):
        def step(t, carry):
            j, c = lax.div(t, 2), pl.multiple_of(256 * lax.rem(t, 2), 256)
            left = H[j, :, :, :, pl.ds(c, 256)].reshape(768, 256)
            got = dot(left, CA[k].reshape(768, 512), 0, 0).reshape(2, 8, 16, 512)
            m = MO[k, pl.ds(2 * t, 2)].astype(F32)
            to(t, (got * m[:, None]).reshape(256, 512).astype(BF))
            return carry
        lax.fori_loop(0, 8, step, 0)

    def far_out(t, v):
        FO[pl.ds(pl.multiple_of(t * 256, 256), 256), :] = v

    def own_out(t, v):
        DO[pl.ds(pl.multiple_of(core * 2048 + t * 256, 256), 256), :] = v

    def in_grad(lo, hi, k, to):
        def step(i, carry):
            d = pl.multiple_of(i * 256, 256)
            left = TA[k, :, :, :, :, :, pl.ds(d, 256)].reshape(768, 256)
            for j in range(CHUNKS):
                got = dot(left, G[j].reshape(768, WIDE), 0, 0).reshape(2, 8, 16, WIDE)
                m = MI[k, pl.ds(2 * i, 2), :, WIDE * j : WIDE * (j + 1)].astype(F32)
                to(d, j, (got * m[:, None]).reshape(256, WIDE).astype(BF))
            return carry
        lax.fori_loop(lo, hi, step, 0)

    def far_in(d, j, v):
        FI[pl.ds(d, 256), WIDE * j : WIDE * (j + 1)] = v

    def own_in(d, j, v):
        DI[pl.ds(d, 256), pl.ds(pl.multiple_of(core * 2048 + WIDE * j, WIDE), WIDE)] = v

    both = range(2)

    def arrived(s, lo, hi):
        for j in range(lo, hi):
            for p in range(PARTS):
                d3[s][j, p].wait_recv()

    arrived(0, 0, 2)
    for k in both:
        for u in both:
            out_part(H, 0, 2, u, k, wout_of, 0)
    arrived(0, 2, 4)
    cross0 = []
    for u in both:
        out_part(H, 2, 4, u, other, wout_of, 0)
        cross0.append(row_cross(0, u))
    for u in units[:6]:
        double_third(1, *u, G)
    for u in both:
        out_part(H, 2, 4, u, core, wout_of, 0)
    for u in units[6:]:
        double_third(1, *u, G)
    pair = [row_first(cross0[u], 0, u) for u in both]
    wo_c.wait_send()
    mo_c.wait_recv()
    out_grad(other, far_out)
    dwo_far = push(FO, DO.at[cols(core)], at_core)
    pair = [row_second(pair[u], 0, u) for u in both]
    out_grad(core, own_out)
    for u in both:
        row_third(pair[u], 0, u)
    for c in cross0:
        c.wait_send()
    arrived(1, 0, 3)
    for k in both:
        for u in both:
            out_part(G, 0, 3, u, k, win_of, 1)
    arrived(1, 3, 4)
    cross1 = []
    for u in both:
        out_part(G, 3, 4, u, other, win_of, 1)
        cross1.append(row_cross(1, u))
    last0 = [row_fourth(0, u) for u in both]
    for u in both:
        out_part(G, 3, 4, u, core, win_of, 1)
    pair = [row_first(cross1[u], 1, u) for u in both]
    wi_c.wait_send()
    mi_c.wait_recv()
    in_grad(0, 2, other, far_in)
    dwi_far = push(FI, DI.at[:, cols(core)], at_core)
    pair = [row_second(pair[u], 1, u) for u in both]
    in_grad(0, 1, core, own_in)
    last1 = []
    for u in both:
        row_third(pair[u], 1, u)
        last1.append(row_fourth(1, u))
    in_grad(1, 2, core, own_in)
    for u in both:
        row_last(last0[u], 0, u, res_o)
    for u in both:
        row_last(last1[u], 1, u, tg_o)
    dwo_far.wait_recv()
    dwi_far.wait_recv()
    waited = [wo_c, wi_c] + cross0
    for c in sent:
        if not any(c is w for w in waited):
            c.wait_send()


def body(tokens, weight_in, mask_in, weight_out, mask_out, cotangent):
    anywhere = pl.BlockSpec(memory_space=pl.ANY)
    vmem = pl.BlockSpec(memory_space=pltpu.VMEM)
    smem = pl.BlockSpec(memory_space=pltpu.SMEM)

    def halving():
        return [
            pltpu.VMEM((CHUNKS, PARTS, 2, 2, 32, WIDE), BF),
            pltpu.VMEM((CHUNKS, PARTS, 2, 2, 32, WIDE), BF),
            pltpu.VMEM((CHUNKS, PARTS, 2, 2, 32, WIDE), F32),
            pltpu.VMEM((CHUNKS, PARTS, 2, 32, WIDE), BF),
            pltpu.VMEM((CHUNKS, PARTS, 2, 32, WIDE), BF),
            pltpu.VMEM((CHUNKS, PARTS, 32, WIDE), BF),
            pltpu.VMEM((CHUNKS, PARTS, 32, WIDE), BF),
        ]

    result, tokens_grad, dwi, dwo = pl.pallas_call(
        kernel,
        out_shape=(
            OUT_KIND((2, 48, 512), BF),
            OUT_KIND((2, 48, 512), BF),
            OUT_KIND((512, 4096), BF),
            OUT_KIND((4096, 512), BF),
        ),
        in_specs=[anywhere] * 4 + [smem] * 2,
        out_specs=(vmem,) * 4,
        scratch_shapes=[
            pltpu.VMEM((2, 2, 2, 2, 2, 48, 512), BF),
            pltpu.VMEM((2, 2, 2, 2, 2, 48, 512), BF),
            pltpu.VMEM((2, 512, 2048), BF),
            pltpu.VMEM((2, 2048, 512), BF),
            pltpu.VMEM((512, 2048), BF),
            pltpu.VMEM((2048, 512), BF),
            pltpu.VMEM((4, 16, 2048), BF),
            pltpu.VMEM((2, 4, 16, 2048), BF),
            pltpu.VMEM((16, 16, 512), BF),
            pltpu.VMEM((2, 16, 16, 512), BF),
        ]
        + halving()
        + halving()
        + [
            pltpu.VMEM((CHUNKS, 8, PARTS, 32, WIDE), BF),
            pltpu.VMEM((CHUNKS, 8, PARTS, 32, WIDE), BF),
            pltpu.VMEM((2, 2, 2, 2, 2, 2, 48, 256), F32),
            pltpu.VMEM((2, 2, 2, 2, 2, 2, 48, 256), F32),
            pltpu.VMEM((2, 2, 2, 2, 2, 48, 256), BF),
            pltpu.VMEM((2, 2, 2, 2, 2, 48, 256), BF),
            pltpu.VMEM((2, 2, 2, 2, 48, 256), BF),
            pltpu.VMEM((2, 2, 2, 2, 48, 256), BF),
            pltpu.VMEM((2, 2, 2, 48, 256), BF),
            pltpu.VMEM((2, 2, 2, 48, 256), BF),
            pltpu.VMEM((2, 2, 2, 48, 256), F32),
            pltpu.SemaphoreType.DMA((N_COPIES,)),
            pltpu.SemaphoreType.DMA((N_COPIES,)),
            pltpu.SemaphoreType.DMA((8,)),
        ],
        compiler_params=pltpu.CompilerParams(
            collective_id=0, has_side_effects=True, vmem_limit_bytes=VMEM_BYTES
        ),
    )(tokens.reshape(2, 48, 512), cotangent.reshape(2, 48, 512), weight_in, weight_out, mask_in, mask_out.T)
    return result.reshape(96, 512), tokens_grad.reshape(96, 512), dwi, dwo


def solution(mesh):
    return jax.shard_map(
        body,
        mesh=mesh,
        in_specs=(
            P("row", "col"),
            P("col", "row"),
            P("col", "row"),
            P("row", "col"),
            P("row", "col"),
            P("row", "col"),
        ),
        out_specs=(P("row", "col"), P("row", "col"), P("col", "row"), P("row", "col")),
        check_vma=False,
    )
```

```python
import jax
import jax.numpy as jnp
from jax import lax
from jax.experimental import pallas as pl
from jax.experimental.pallas import tpu as pltpu
from jax.sharding import PartitionSpec as P

BLOCK = 128
CHUNKS = 4
WIDE = 512
BF = jnp.bfloat16
F32 = jnp.float32

root_two_pi = 0.7978845608
cubic_coef = 0.044715

ORDERS = ((0, 1, 2), (1, 2, 0), (2, 0, 1))
PARTS = 3


def order(j, p):
    return ORDERS[(j + p) % 3]


def dot(left, right, left_dim, right_dim):
    return lax.dot_general(
        left, right, (((left_dim,), (right_dim,)), ((), ())), preferred_element_type=F32
    )


def gelu_both(values):
    tangent = jnp.tanh(root_two_pi * (values + cubic_coef * values * values * values))
    value = 0.5 * values * (1.0 + tangent)
    slope = 0.5 * (1.0 + tangent) + 0.5 * values * (1.0 - tangent * tangent) * root_two_pi * (
        1.0 + 3.0 * cubic_coef * values * values
    )
    return value, slope
OUT_KIND = pltpu.VMEM
VMEM_BYTES = 53 * 1024 * 1024


N_COPIES = 256


def kernel(
    tok, cot, win, wout, mask_in, mask_out_t,
    res_o, tg_o, DI, DO,
    TA, CA, WI, WO, FI, FO, MIS, MI, MOS, MO,
    S1a, R1a, ACa, S2a, R2a, S3a, R3a,
    S1b, R1b, ACb, S2b, R2b, S3b, R3b,
    H, G, R, RX, T1, U1, T2, U2, T3, U3, KEEP,
    send_sem, recv_sem, local_sem,
):
    row = lax.axis_index("row")
    col = lax.axis_index("col")
    x, yh = lax.div(row, 2), lax.rem(row, 2)
    yl = lax.div(col, 8)
    z = lax.div(lax.rem(col, 8), 2)
    core = lax.rem(col, 2)
    other = 1 - core
    xb, xa = lax.div(x, 2), lax.rem(lax.div(x + 1, 2), 2)
    zb, za = lax.div(z, 2), lax.rem(lax.div(z + 1, 2), 2)
    at_core = {"row": row, "col": col + 1 - 2 * core}
    at_y = {"row": row, "col": col + 8 - 16 * yl}
    at_za = {"row": row, "col": col + 2 * (1 - 2 * lax.rem(z, 2))}
    at_zb = {"row": row, "col": col + 2 * (3 - 2 * z)}
    at_xa = {"row": row + 2 * (1 - 2 * lax.rem(x, 2)), "col": col}
    at_xb = {"row": row + 2 * (3 - 2 * x), "col": col}
    at_yh = {"row": row + 1 - 2 * yh, "col": col}
    bits = (yl, za, zb)
    partner = (at_y, at_za, at_zb)

    count = [0]
    sent = []

    def push(src, dst, where):
        k = count[0]
        count[0] += 1
        copy = pltpu.make_async_remote_copy(
            src_ref=src, dst_ref=dst, send_sem=send_sem.at[k], recv_sem=recv_sem.at[k],
            device_id=where, device_id_type=pl.DeviceIdType.MESH,
        )
        copy.start()
        sent.append(copy)
        return copy

    lcount = [0]

    def local(src, dst):
        k = lcount[0]
        lcount[0] += 1
        copy = pltpu.make_async_copy(src, dst, local_sem.at[k])
        copy.start()
        return copy

    def cols(h):
        return pl.ds(pl.multiple_of(h * 2048, 2048), 2048)

    barrier = pltpu.get_barrier_semaphore()
    for where in (at_core, at_y, at_za, at_zb, at_xa, at_xb, at_yh):
        pl.semaphore_signal(barrier, inc=1, device_id=where, device_id_type=pl.DeviceIdType.MESH)

    tok_in = local(tok, TA.at[core, xb, xa, yh])
    cot_in = local(cot, CA.at[core, xb, xa, yh])
    si_far = local(win.at[:, cols(other)], DI.at[:, cols(other)])
    si_own = local(win.at[:, cols(core)], DI.at[:, cols(core)])
    so_far = local(wout.at[cols(other)], DO.at[cols(other)])
    so_own = local(wout.at[cols(core)], DO.at[cols(core)])

    def spread(scalar):
        return jnp.full((16, BLOCK), scalar.astype(F32), F32).astype(BF)

    def expand_in(h, dst):
        def step(j, carry):
            for i in range(4):
                dst[i, :, pl.ds(pl.multiple_of(j * BLOCK, BLOCK), BLOCK)] = spread(
                    mask_in[i, h * 16 + j]
                )
            return carry
        lax.fori_loop(0, 16, step, 0)

    def expand_out(h, dst):
        def step(i, carry):
            for j in range(4):
                dst[i, :, BLOCK * j : BLOCK * (j + 1)] = spread(mask_out_t[j, h * 16 + i])
            return carry
        lax.fori_loop(0, 16, step, 0)

    expand_in(other, MIS)
    expand_in(core, MI.at[core])
    expand_out(other, MOS)
    expand_out(core, MO.at[core])
    pl.semaphore_wait(barrier, 7)

    def gather_y(A, c):
        for hf in range(2):
            at = A.at[core, xb, xa, yh, hf]
            c["y%d" % hf] = push(at, at, at_yh)

    def gather_first(A, c):
        c["a0"] = push(A.at[core, xb, xa, yh, 0], A.at[core, xb, xa, yh, 0], at_xb)
        c["b0"] = push(A.at[core, xb, xa, yh, 1], A.at[core, xb, xa, yh, 1], at_xa)

    def gather_second(A, c, v, tag):
        c["a" + tag].wait_recv()
        c["A" + tag] = push(A.at[core, :, xa, v, 0], A.at[core, :, xa, v, 0], at_xa)
        c["b" + tag].wait_recv()
        c["B" + tag] = push(A.at[core, xb, :, v, 1], A.at[core, xb, :, v, 1], at_xb)

    def gather_third(A, c, v):
        c["y0"].wait_recv()
        c["a1"] = push(A.at[core, xb, xa, v, 0], A.at[core, xb, xa, v, 0], at_xb)
        c["y1"].wait_recv()
        c["b1"] = push(A.at[core, xb, xa, v, 1], A.at[core, xb, xa, v, 1], at_xa)

    def gather_cross(A, c, v, tag):
        c["A" + tag].wait_recv()
        one = push(A.at[core, :, :, v, 0], A.at[core, :, :, v, 0], at_core)
        c["B" + tag].wait_recv()
        two = push(A.at[core, :, :, v, 1], A.at[core, :, :, v, 1], at_core)
        c["c" + tag] = (one, two)

    def crossed(c, tag):
        for copy in c["c" + tag]:
            copy.wait_recv()

    def mask_in_half(h, m, dst):
        def step(i, carry):
            r = pl.multiple_of(i * BLOCK, BLOCK)
            w = DI[pl.ds(r, BLOCK), cols(h)].reshape(8, 16, 2048)
            dst[pl.ds(r, BLOCK), :] = (w * m[i][None]).reshape(BLOCK, 2048)
            return carry
        lax.fori_loop(0, 4, step, 0)

    def mask_out_half(h, m, dst):
        def step(i, carry):
            r = pl.multiple_of(i * BLOCK, BLOCK)
            w = DO[pl.ds(pl.multiple_of(h * 2048 + r, BLOCK), BLOCK), :].reshape(8, 16, 512)
            dst[pl.ds(r, BLOCK), :] = (w * m[i][None]).reshape(BLOCK, 512)
            return carry
        lax.fori_loop(0, 16, step, 0)

    tok_in.wait()
    tc, cc = {}, {}
    gather_y(TA, tc)
    gather_first(TA, tc)
    si_far.wait()
    mask_in_half(other, MIS, FI)
    wi_c = push(FI, WI.at[core], at_core)
    gather_second(TA, tc, yh, "0")
    cot_in.wait()
    gather_first(CA, cc)
    si_own.wait()
    mask_in_half(core, MI.at[core], WI.at[core])
    gather_third(TA, tc, 1 - yh)
    gather_y(CA, cc)
    gather_cross(TA, tc, yh, "0")
    so_far.wait()
    mask_out_half(other, MOS, FO)
    wo_c = push(FO, WO.at[core], at_core)
    wi_c.wait_recv()
    crossed(tc, "0")

    def part_in(j, v):
        out = None
        for k in range(2):
            t = dot(TA[k, :, :, v].reshape(384, 512), WI[k, :, WIDE * j : WIDE * (j + 1)], 1, 0)
            out = t if out is None else out + t
        return out.reshape(2, 2, PARTS, 32, WIDE)

    def part_out(j, v):
        out = None
        for k in range(2):
            t = dot(CA[k, :, :, v].reshape(384, 512), WO[k, WIDE * j : WIDE * (j + 1), :], 1, 1)
            out = t if out is None else out + t
        return out.reshape(2, 2, PARTS, 32, WIDE)

    streams = ((part_in, S1a, R1a, ACa, S2a, R2a, S3a, R3a), (part_out, S1b, R1b, ACb, S2b, R2b, S3b, R3b))
    units = [(j, p) for j in range(CHUNKS) for p in range(PARTS)]
    parted = [(j, p) for p in range(PARTS) for j in range(CHUNKS)]
    first = [{u: () for u in units} for _ in range(2)]
    second, third = [{}, {}], [{}, {}]

    def halve_first(s, j, v):
        part, S1, R1, AC, S2, R2, S3, R3 = streams[s]
        got = part(j, v)
        for p in range(PARTS):
            d = order(j, p)[0]
            low = bits[d] == 0
            S1[j, p, :, v] = jnp.where(low, got[1, :, p], got[0, :, p]).astype(BF)
            c = push(S1.at[j, p, :, v], R1.at[j, p, :, v], partner[d])
            first[s][j, p] += (c,)
        for p in range(PARTS):
            low = bits[order(j, p)[0]] == 0
            AC[j, p, :, v] = jnp.where(low, got[0, :, p], got[1, :, p])

    def halve_second(s, j, p):
        part, S1, R1, AC, S2, R2, S3, R3 = streams[s]
        d = order(j, p)[1]
        away, keep = 1 - bits[d], bits[d]
        for c in first[s][j, p]:
            c.wait_recv()
        S2[j, p] = (AC[j, p, away] + R1[j, p, away].astype(F32)).astype(BF)
        second[s][j, p] = push(S2.at[j, p], R2.at[j, p], partner[d])
        AC[j, p, keep] = AC[j, p, keep] + R1[j, p, keep].astype(F32)

    def halve_third(s, j, p):
        part, S1, R1, AC, S2, R2, S3, R3 = streams[s]
        base, d = bits[order(j, p)[1]], order(j, p)[2]
        away, keep = 1 - bits[d], bits[d]
        second[s][j, p].wait_recv()
        S3[j, p] = (AC[j, p, base, away] + R2[j, p, away].astype(F32)).astype(BF)
        third[s][j, p] = push(S3.at[j, p], R3.at[j, p], partner[d])
        AC[j, p, base, keep] = AC[j, p, base, keep] + R2[j, p, keep].astype(F32)

    def whole(s, j, p):
        part, S1, R1, AC, S2, R2, S3, R3 = streams[s]
        third[s][j, p].wait_recv()
        base, last = bits[order(j, p)[1]], bits[order(j, p)[2]]
        return AC[j, p, base, last] + R3[j, p].astype(F32), base, last

    d1, d2, d3 = [{}, {}], [{}, {}], [{}, {}]

    def double_first(s, j, p, A):
        m = [bits[d] for d in order(j, p)]
        at = A.at[j, 4 * m[0] + 2 * m[1] + m[2], p]
        d1[s][j, p] = push(at, at, partner[order(j, p)[2]])

    def double_second(s, j, p, A):
        m = [bits[d] for d in order(j, p)]
        d1[s][j, p].wait_recv()
        at = A.at[j, pl.ds(4 * m[0] + 2 * m[1], 2), p]
        d2[s][j, p] = push(at, at, partner[order(j, p)[1]])

    def double_third(s, j, p, A):
        m = [bits[d] for d in order(j, p)]
        d2[s][j, p].wait_recv()
        at = A.at[j, pl.ds(4 * m[0], 4), p]
        d3[s][j, p] = push(at, at, partner[order(j, p)[0]])

    def make_hidden(j, p):
        m = [bits[d] for d in order(j, p)]
        v, base, last = whole(0, j, p)
        value, slope = gelu_both(v)
        H[j, 4 * m[0] + 2 * m[1] + m[2], p] = value.astype(BF)
        ACa[j, p, base, last] = slope
        double_first(0, j, p, H)

    def make_grad(j, p):
        m = [bits[d] for d in order(j, p)]
        v, base, last = whole(1, j, p)
        G[j, 4 * m[0] + 2 * m[1] + m[2], p] = (v * ACa[j, p, base, last]).astype(BF)
        double_first(1, j, p, G)

    far = 1 - yh
    halve_first(0, 0, yh)
    gather_second(TA, tc, far, "1")
    halve_first(0, 1, yh)
    gather_second(CA, cc, yh, "0")
    halve_first(0, 2, yh)
    so_own.wait()
    mask_out_half(core, MO.at[core], WO.at[core])
    halve_first(0, 3, yh)
    gather_cross(CA, cc, yh, "0")
    gather_cross(TA, tc, far, "1")
    wo_c.wait_recv()
    crossed(cc, "0")
    halve_first(1, 0, yh)
    gather_third(CA, cc, far)
    halve_first(1, 1, yh)
    mi_c = push(MIS, MI.at[core], at_core)
    mo_c = push(MOS, MO.at[core], at_core)
    halve_first(1, 2, yh)
    gather_second(CA, cc, far, "1")
    halve_first(1, 3, yh)
    crossed(tc, "1")
    halve_first(0, 0, far)
    halve_first(0, 1, far)
    gather_cross(CA, cc, far, "1")
    halve_first(0, 2, far)
    halve_first(0, 3, far)
    crossed(cc, "1")
    for j in range(CHUNKS):
        halve_first(1, j, far)
    for u in units:
        halve_second(0, *u)
    for u in units:
        halve_third(0, *u)
    for u in units:
        halve_second(1, *u)
    for u in parted:
        make_hidden(*u)
    for u in units:
        halve_third(1, *u)
    for u in parted:
        double_second(0, *u, H)
    for u in parted:
        make_grad(*u)
    for u in parted:
        double_third(0, *u, H)
    for u in parted:
        double_second(1, *u, G)

    every = slice(None)

    def out_part(A, p, k, weight, right_dim):
        left = jnp.concatenate([A[i, :, p].reshape(256, WIDE) for i in range(CHUNKS)], axis=1)
        R[k, p] = dot(left, weight[k], 1, right_dim).reshape(2, 2, 2, 2, 16, 512)

    def row_cross(n, p):
        return push(R.at[other, p], RX.at[n, p], at_core)

    def full(n, p, idx):
        return R[(core, p) + idx] + RX[(n, p) + idx]

    def row_first(cross, n, p):
        cross.wait_recv()
        T1[n, p, 0] = full(n, p, (1 - xb, every, every, 0)).astype(BF)
        a = push(T1.at[n, p, 0], U1.at[n, p, 0], at_xb)
        T1[n, p, 1] = full(n, p, (every, 1 - xa, every, 1)).astype(BF)
        b = push(T1.at[n, p, 1], U1.at[n, p, 1], at_xa)
        return a, b

    def row_second(copies, n, p):
        copies[0].wait_recv()
        T2[n, p, 0] = (full(n, p, (xb, 1 - xa, every, 0)) + U1[n, p, 0, 1 - xa].astype(F32)).astype(BF)
        a = push(T2.at[n, p, 0], U2.at[n, p, 0], at_xa)
        copies[1].wait_recv()
        T2[n, p, 1] = (full(n, p, (1 - xb, xa, every, 1)) + U1[n, p, 1, 1 - xb].astype(F32)).astype(BF)
        b = push(T2.at[n, p, 1], U2.at[n, p, 1], at_xb)
        return a, b

    def row_third(copies, n, p):
        def row_sum(v, hf):
            near = (xa, xb)[hf]
            return (
                full(n, p, (xb, xa, v, hf))
                + U1[n, p, hf, near, v].astype(F32)
                + U2[n, p, hf, v].astype(F32)
            )

        for hf in range(2):
            copies[hf].wait_recv()
            T3[n, p, hf] = row_sum(1 - yh, hf).astype(BF)
            KEEP[n, p, hf] = row_sum(yh, hf)

    def row_fourth(n, p):
        return push(T3.at[n, p], U3.at[n, p], at_yh)

    def row_last(copy, n, p, out):
        copy.wait_recv()
        out[p] = (KEEP[n, p] + U3[n, p].astype(F32)).astype(BF)

    def out_grad(k, to):
        def step(t, carry):
            j, c = lax.div(t, 2), pl.multiple_of(256 * lax.rem(t, 2), 256)
            left = H[j, :, :, :, pl.ds(c, 256)].reshape(768, 256)
            got = dot(left, CA[k].reshape(768, 512), 0, 0).reshape(2, 8, 16, 512)
            m = MO[k, pl.ds(2 * t, 2)].astype(F32)
            to(t, (got * m[:, None]).reshape(256, 512).astype(BF))
            return carry
        lax.fori_loop(0, 8, step, 0)

    def far_out(t, v):
        FO[pl.ds(pl.multiple_of(t * 256, 256), 256), :] = v

    def own_out(t, v):
        DO[pl.ds(pl.multiple_of(core * 2048 + t * 256, 256), 256), :] = v

    def in_grad(lo, hi, k, to):
        def step(i, carry):
            d = pl.multiple_of(i * 256, 256)
            left = TA[k, :, :, :, :, :, pl.ds(d, 256)].reshape(768, 256)
            for j in range(CHUNKS):
                got = dot(left, G[j].reshape(768, WIDE), 0, 0).reshape(2, 8, 16, WIDE)
                m = MI[k, pl.ds(2 * i, 2), :, WIDE * j : WIDE * (j + 1)].astype(F32)
                to(d, j, (got * m[:, None]).reshape(256, WIDE).astype(BF))
            return carry
        lax.fori_loop(lo, hi, step, 0)

    def far_in(d, j, v):
        FI[pl.ds(d, 256), WIDE * j : WIDE * (j + 1)] = v

    def own_in(d, j, v):
        DI[pl.ds(d, 256), pl.ds(pl.multiple_of(core * 2048 + WIDE * j, WIDE), WIDE)] = v

    def arrived(s, p):
        for j in range(CHUNKS):
            d3[s][j, p].wait_recv()

    cross0, cross1, pair0, pair1 = {}, {}, {}, {}

    def third_of(p):
        for j in range(CHUNKS):
            double_third(1, j, p, G)

    for p in range(PARTS):
        arrived(0, p)
        out_part(H, p, other, WO, 0)
        cross0[p] = row_cross(0, p)
        if p == 2:
            third_of(0)
        out_part(H, p, core, WO, 0)
    third_of(1)
    pair0[0] = row_first(cross0[0], 0, 0)
    third_of(2)
    for p in (1, 2):
        pair0[p] = row_first(cross0[p], 0, p)
    wo_c.wait_send()
    mo_c.wait_recv()
    out_grad(other, far_out)
    dwo_far = push(FO, DO.at[cols(core)], at_core)
    for p in range(PARTS):
        pair0[p] = row_second(pair0[p], 0, p)
    out_grad(core, own_out)
    for p in range(PARTS):
        row_third(pair0[p], 0, p)
        cross0[p].wait_send()

    def row_part(p):
        arrived(1, p)
        out_part(G, p, other, WI, 1)
        cross1[p] = row_cross(1, p)

    row_part(0)
    out_part(G, 0, core, WI, 1)
    row_part(1)
    pair1[0] = row_first(cross1[0], 1, 0)
    out_part(G, 1, core, WI, 1)
    row_part(2)
    last0 = [row_fourth(0, p) for p in range(PARTS)]
    pair1[1] = row_first(cross1[1], 1, 1)
    out_part(G, 2, core, WI, 1)
    pair1[0] = row_second(pair1[0], 1, 0)
    pair1[2] = row_first(cross1[2], 1, 2)
    wi_c.wait_send()
    mi_c.wait_recv()
    in_grad(0, 1, other, far_in)
    pair1[1] = row_second(pair1[1], 1, 1)
    row_third(pair1[0], 1, 0)
    last1 = [row_fourth(1, 0)]
    in_grad(1, 2, other, far_in)
    dwi_far = push(FI, DI.at[:, cols(core)], at_core)
    pair1[2] = row_second(pair1[2], 1, 2)
    row_third(pair1[1], 1, 1)
    last1.append(row_fourth(1, 1))
    in_grad(0, 1, core, own_in)
    row_third(pair1[2], 1, 2)
    last1.append(row_fourth(1, 2))
    in_grad(1, 2, core, own_in)
    for p in range(PARTS):
        row_last(last0[p], 0, p, res_o)
    for p in range(PARTS):
        row_last(last1[p], 1, p, tg_o)
    dwo_far.wait_recv()
    dwi_far.wait_recv()
    waited = [wo_c, wi_c] + list(cross0.values())
    for c in sent:
        if not any(c is w for w in waited):
            c.wait_send()


def leave(a, b, c, d, a_o, b_o, c_o, d_o, sem):
    copies = [
        pltpu.make_async_copy(src, dst, sem.at[k])
        for k, (src, dst) in enumerate(((c, c_o), (d, d_o), (a, a_o), (b, b_o)))
    ]
    for copy in copies:
        copy.start()
    for copy in copies:
        copy.wait()


def body(tokens, weight_in, mask_in, weight_out, mask_out, cotangent):
    anywhere = pl.BlockSpec(memory_space=pl.ANY)
    vmem = pl.BlockSpec(memory_space=pltpu.VMEM)
    smem = pl.BlockSpec(memory_space=pltpu.SMEM)

    def halving():
        return [
            pltpu.VMEM((CHUNKS, PARTS, 2, 2, 32, WIDE), BF),
            pltpu.VMEM((CHUNKS, PARTS, 2, 2, 32, WIDE), BF),
            pltpu.VMEM((CHUNKS, PARTS, 2, 2, 32, WIDE), F32),
            pltpu.VMEM((CHUNKS, PARTS, 2, 32, WIDE), BF),
            pltpu.VMEM((CHUNKS, PARTS, 2, 32, WIDE), BF),
            pltpu.VMEM((CHUNKS, PARTS, 32, WIDE), BF),
            pltpu.VMEM((CHUNKS, PARTS, 32, WIDE), BF),
        ]

    held = pl.pallas_call(
        kernel,
        out_shape=(
            OUT_KIND((PARTS, 2, 16, 512), BF),
            OUT_KIND((PARTS, 2, 16, 512), BF),
            OUT_KIND((512, 4096), BF),
            OUT_KIND((4096, 512), BF),
        ),
        in_specs=[anywhere] * 4 + [smem] * 2,
        out_specs=(vmem,) * 4,
        scratch_shapes=[
            pltpu.VMEM((2, 2, 2, 2, 2, 48, 512), BF),
            pltpu.VMEM((2, 2, 2, 2, 2, 48, 512), BF),
            pltpu.VMEM((2, 512, 2048), BF),
            pltpu.VMEM((2, 2048, 512), BF),
            pltpu.VMEM((512, 2048), BF),
            pltpu.VMEM((2048, 512), BF),
            pltpu.VMEM((4, 16, 2048), BF),
            pltpu.VMEM((2, 4, 16, 2048), BF),
            pltpu.VMEM((16, 16, 512), BF),
            pltpu.VMEM((2, 16, 16, 512), BF),
        ]
        + halving()
        + halving()
        + [
            pltpu.VMEM((CHUNKS, 8, PARTS, 32, WIDE), BF),
            pltpu.VMEM((CHUNKS, 8, PARTS, 32, WIDE), BF),
            pltpu.VMEM((2, PARTS, 2, 2, 2, 2, 16, 512), F32),
            pltpu.VMEM((2, PARTS, 2, 2, 2, 2, 16, 512), F32),
            pltpu.VMEM((2, PARTS, 2, 2, 2, 16, 512), BF),
            pltpu.VMEM((2, PARTS, 2, 2, 2, 16, 512), BF),
            pltpu.VMEM((2, PARTS, 2, 2, 16, 512), BF),
            pltpu.VMEM((2, PARTS, 2, 2, 16, 512), BF),
            pltpu.VMEM((2, PARTS, 2, 16, 512), BF),
            pltpu.VMEM((2, PARTS, 2, 16, 512), BF),
            pltpu.VMEM((2, PARTS, 2, 16, 512), F32),
            pltpu.SemaphoreType.DMA((N_COPIES,)),
            pltpu.SemaphoreType.DMA((N_COPIES,)),
            pltpu.SemaphoreType.DMA((8,)),
        ],
        compiler_params=pltpu.CompilerParams(
            collective_id=0, has_side_effects=True, vmem_limit_bytes=VMEM_BYTES
        ),
    )(tokens.reshape(2, 48, 512), cotangent.reshape(2, 48, 512), weight_in, weight_out, mask_in, mask_out.T)
    shapes = ((PARTS, 2, 16, 512), (PARTS, 2, 16, 512), (512, 4096), (4096, 512))
    result, tokens_grad, dwi, dwo = pl.pallas_call(
        leave,
        out_shape=tuple(jax.ShapeDtypeStruct(shape, BF) for shape in shapes),
        in_specs=[anywhere] * 4,
        out_specs=(anywhere,) * 4,
        scratch_shapes=[pltpu.SemaphoreType.DMA((4,))],
        compiler_params=pltpu.CompilerParams(vmem_limit_bytes=1024 * 1024),
    )(*held)
    return result.reshape(96, 512), tokens_grad.reshape(96, 512), dwi, dwo


def solution(mesh):
    return jax.shard_map(
        body,
        mesh=mesh,
        in_specs=(
            P("row", "col"),
            P("col", "row"),
            P("col", "row"),
            P("row", "col"),
            P("row", "col"),
            P("row", "col"),
        ),
        out_specs=(P("row", "col"), P("row", "col"), P("col", "row"), P("row", "col")),
        check_vma=False,
    )
```

```python
import jax
import jax.numpy as jnp
from jax import lax
from jax.experimental import pallas as pl
from jax.experimental.pallas import tpu as pltpu
from jax.sharding import PartitionSpec as P

BLOCK = 128
CHUNKS = 4
WIDE = 512
BF = jnp.bfloat16
F32 = jnp.float32

root_two_pi = 0.7978845608
cubic_coef = 0.044715

ORDERS = ((0, 1, 2), (1, 2, 0), (2, 0, 1))
PARTS = 3


def order(j, p):
    return ORDERS[(j + p) % 3]


def dot(left, right, left_dim, right_dim):
    return lax.dot_general(
        left, right, (((left_dim,), (right_dim,)), ((), ())), preferred_element_type=F32
    )


def gelu_both(values):
    tangent = jnp.tanh(root_two_pi * (values + cubic_coef * values * values * values))
    value = 0.5 * values * (1.0 + tangent)
    slope = 0.5 * (1.0 + tangent) + 0.5 * values * (1.0 - tangent * tangent) * root_two_pi * (
        1.0 + 3.0 * cubic_coef * values * values
    )
    return value, slope
OUT_KIND = pltpu.VMEM
VMEM_BYTES = 53 * 1024 * 1024


N_COPIES = 256


def kernel(
    tok, cot, win, wout, mask_in, mask_out_t,
    res_o, tg_o, DI, DO,
    TA, CA, WI, WO, FI, FO, MIS, MI, MOS, MO,
    S1a, R1a, ACa, S2a, R2a, S3a, R3a,
    S1b, R1b, ACb, S2b, R2b, S3b, R3b,
    H, G, R, RX, T1, U1, T2, U2, T3, U3, KEEP,
    send_sem, recv_sem, local_sem,
):
    row = lax.axis_index("row")
    col = lax.axis_index("col")
    x, yh = lax.div(row, 2), lax.rem(row, 2)
    yl = lax.div(col, 8)
    z = lax.div(lax.rem(col, 8), 2)
    core = lax.rem(col, 2)
    other = 1 - core
    xb, xa = lax.div(x, 2), lax.rem(lax.div(x + 1, 2), 2)
    zb, za = lax.div(z, 2), lax.rem(lax.div(z + 1, 2), 2)
    at_core = {"row": row, "col": col + 1 - 2 * core}
    at_y = {"row": row, "col": col + 8 - 16 * yl}
    at_za = {"row": row, "col": col + 2 * (1 - 2 * lax.rem(z, 2))}
    at_zb = {"row": row, "col": col + 2 * (3 - 2 * z)}
    at_xa = {"row": row + 2 * (1 - 2 * lax.rem(x, 2)), "col": col}
    at_xb = {"row": row + 2 * (3 - 2 * x), "col": col}
    at_yh = {"row": row + 1 - 2 * yh, "col": col}
    bits = (yl, za, zb)
    partner = (at_y, at_za, at_zb)

    count = [0]
    sent = []

    def push(src, dst, where):
        k = count[0]
        count[0] += 1
        copy = pltpu.make_async_remote_copy(
            src_ref=src, dst_ref=dst, send_sem=send_sem.at[k], recv_sem=recv_sem.at[k],
            device_id=where, device_id_type=pl.DeviceIdType.MESH,
        )
        copy.start()
        sent.append(copy)
        return copy

    lcount = [0]

    def local(src, dst):
        k = lcount[0]
        lcount[0] += 1
        copy = pltpu.make_async_copy(src, dst, local_sem.at[k])
        copy.start()
        return copy

    def cols(h):
        return pl.ds(pl.multiple_of(h * 2048, 2048), 2048)

    barrier = pltpu.get_barrier_semaphore()
    for where in (at_core, at_y, at_za, at_zb, at_xa, at_xb, at_yh):
        pl.semaphore_signal(barrier, inc=1, device_id=where, device_id_type=pl.DeviceIdType.MESH)

    tok_in = local(tok, TA.at[core, xb, xa, yh])
    cot_in = local(cot, CA.at[core, xb, xa, yh])
    si_far = local(win.at[:, cols(other)], DI.at[:, cols(other)])
    si_own = local(win.at[:, cols(core)], DI.at[:, cols(core)])
    so_far = local(wout.at[cols(other)], DO.at[cols(other)])
    so_own = local(wout.at[cols(core)], DO.at[cols(core)])

    def spread(scalar):
        return jnp.full((16, BLOCK), scalar.astype(F32), F32).astype(BF)

    def expand_in(h, dst):
        def step(j, carry):
            for i in range(4):
                dst[i, :, pl.ds(pl.multiple_of(j * BLOCK, BLOCK), BLOCK)] = spread(
                    mask_in[i, h * 16 + j]
                )
            return carry
        lax.fori_loop(0, 16, step, 0)

    def expand_out(h, dst):
        def step(i, carry):
            for j in range(4):
                dst[i, :, BLOCK * j : BLOCK * (j + 1)] = spread(mask_out_t[j, h * 16 + i])
            return carry
        lax.fori_loop(0, 16, step, 0)

    expand_in(other, MIS)
    expand_in(core, MI.at[core])
    expand_out(other, MOS)
    expand_out(core, MO.at[core])
    pl.semaphore_wait(barrier, 7)

    def gather_y(A, c):
        for hf in range(2):
            at = A.at[core, xb, xa, yh, hf]
            c["y%d" % hf] = push(at, at, at_yh)

    def gather_first(A, c):
        c["a0"] = push(A.at[core, xb, xa, yh, 0], A.at[core, xb, xa, yh, 0], at_xb)
        c["b0"] = push(A.at[core, xb, xa, yh, 1], A.at[core, xb, xa, yh, 1], at_xa)

    def gather_second(A, c, v, tag):
        c["a" + tag].wait_recv()
        c["A" + tag] = push(A.at[core, :, xa, v, 0], A.at[core, :, xa, v, 0], at_xa)
        c["b" + tag].wait_recv()
        c["B" + tag] = push(A.at[core, xb, :, v, 1], A.at[core, xb, :, v, 1], at_xb)

    def gather_third(A, c, v):
        c["y0"].wait_recv()
        c["a1"] = push(A.at[core, xb, xa, v, 0], A.at[core, xb, xa, v, 0], at_xb)
        c["y1"].wait_recv()
        c["b1"] = push(A.at[core, xb, xa, v, 1], A.at[core, xb, xa, v, 1], at_xa)

    def gather_cross(A, c, v, tag):
        c["A" + tag].wait_recv()
        one = push(A.at[core, :, :, v, 0], A.at[core, :, :, v, 0], at_core)
        c["B" + tag].wait_recv()
        two = push(A.at[core, :, :, v, 1], A.at[core, :, :, v, 1], at_core)
        c["c" + tag] = (one, two)

    def crossed(c, tag):
        for copy in c["c" + tag]:
            copy.wait_recv()

    def mask_in_half(h, m, dst):
        def step(i, carry):
            r = pl.multiple_of(i * BLOCK, BLOCK)
            w = DI[pl.ds(r, BLOCK), cols(h)].reshape(8, 16, 2048)
            dst[pl.ds(r, BLOCK), :] = (w * m[i][None]).reshape(BLOCK, 2048)
            return carry
        lax.fori_loop(0, 4, step, 0)

    def mask_out_half(h, m, dst):
        def step(i, carry):
            r = pl.multiple_of(i * BLOCK, BLOCK)
            w = DO[pl.ds(pl.multiple_of(h * 2048 + r, BLOCK), BLOCK), :].reshape(8, 16, 512)
            dst[pl.ds(r, BLOCK), :] = (w * m[i][None]).reshape(BLOCK, 512)
            return carry
        lax.fori_loop(0, 16, step, 0)

    far = 1 - yh
    tok_in.wait()
    tc, cc = {}, {}
    gather_y(TA, tc)
    gather_first(TA, tc)
    cot_in.wait()
    gather_y(CA, cc)
    si_far.wait()
    mask_in_half(other, MIS, FI)
    wi_c = push(FI, WI.at[core], at_core)
    gather_second(TA, tc, yh, "0")
    gather_first(CA, cc)
    si_own.wait()
    mask_in_half(core, MI.at[core], WI.at[core])
    gather_cross(TA, tc, yh, "0")
    gather_second(CA, cc, yh, "0")
    so_far.wait()
    mask_out_half(other, MOS, FO)
    wo_c = push(FO, WO.at[core], at_core)
    wi_c.wait_recv()
    crossed(tc, "0")

    def part_in(j, v):
        out = None
        for k in range(2):
            t = dot(TA[k, :, :, v].reshape(384, 512), WI[k, :, WIDE * j : WIDE * (j + 1)], 1, 0)
            out = t if out is None else out + t
        return out.reshape(2, 2, PARTS, 32, WIDE)

    def part_out(j, v):
        out = None
        for k in range(2):
            t = dot(CA[k, :, :, v].reshape(384, 512), WO[k, WIDE * j : WIDE * (j + 1), :], 1, 1)
            out = t if out is None else out + t
        return out.reshape(2, 2, PARTS, 32, WIDE)

    streams = ((part_in, S1a, R1a, ACa, S2a, R2a, S3a, R3a), (part_out, S1b, R1b, ACb, S2b, R2b, S3b, R3b))
    units = [(j, p) for j in range(CHUNKS) for p in range(PARTS)]
    parted = [(j, p) for p in range(PARTS) for j in range(CHUNKS)]
    first = [{u: () for u in units} for _ in range(2)]
    second, third = [{}, {}], [{}, {}]

    def halve_first(s, j, v):
        part, S1, R1, AC, S2, R2, S3, R3 = streams[s]
        got = part(j, v)
        for p in range(PARTS):
            d = order(j, p)[0]
            low = bits[d] == 0
            S1[j, p, :, v] = jnp.where(low, got[1, :, p], got[0, :, p]).astype(BF)
            c = push(S1.at[j, p, :, v], R1.at[j, p, :, v], partner[d])
            first[s][j, p] += (c,)
        for p in range(PARTS):
            low = bits[order(j, p)[0]] == 0
            AC[j, p, :, v] = jnp.where(low, got[0, :, p], got[1, :, p])

    def halve_second(s, j, p):
        part, S1, R1, AC, S2, R2, S3, R3 = streams[s]
        d = order(j, p)[1]
        away, keep = 1 - bits[d], bits[d]
        for c in first[s][j, p]:
            c.wait_recv()
        S2[j, p] = (AC[j, p, away] + R1[j, p, away].astype(F32)).astype(BF)
        second[s][j, p] = push(S2.at[j, p], R2.at[j, p], partner[d])
        AC[j, p, keep] = AC[j, p, keep] + R1[j, p, keep].astype(F32)

    def halve_third(s, j, p):
        part, S1, R1, AC, S2, R2, S3, R3 = streams[s]
        base, d = bits[order(j, p)[1]], order(j, p)[2]
        away, keep = 1 - bits[d], bits[d]
        second[s][j, p].wait_recv()
        S3[j, p] = (AC[j, p, base, away] + R2[j, p, away].astype(F32)).astype(BF)
        third[s][j, p] = push(S3.at[j, p], R3.at[j, p], partner[d])
        AC[j, p, base, keep] = AC[j, p, base, keep] + R2[j, p, keep].astype(F32)

    def whole(s, j, p):
        part, S1, R1, AC, S2, R2, S3, R3 = streams[s]
        third[s][j, p].wait_recv()
        base, last = bits[order(j, p)[1]], bits[order(j, p)[2]]
        return AC[j, p, base, last] + R3[j, p].astype(F32), base, last

    d1, d2, d3 = [{}, {}], [{}, {}], [{}, {}]

    def double_first(s, j, p, A):
        m = [bits[d] for d in order(j, p)]
        at = A.at[j, 4 * m[0] + 2 * m[1] + m[2], p]
        d1[s][j, p] = push(at, at, partner[order(j, p)[2]])

    def double_second(s, j, p, A):
        m = [bits[d] for d in order(j, p)]
        d1[s][j, p].wait_recv()
        at = A.at[j, pl.ds(4 * m[0] + 2 * m[1], 2), p]
        d2[s][j, p] = push(at, at, partner[order(j, p)[1]])

    def double_third(s, j, p, A):
        m = [bits[d] for d in order(j, p)]
        d2[s][j, p].wait_recv()
        at = A.at[j, pl.ds(4 * m[0], 4), p]
        d3[s][j, p] = push(at, at, partner[order(j, p)[0]])

    def make_hidden(j, p):
        m = [bits[d] for d in order(j, p)]
        v, base, last = whole(0, j, p)
        value, slope = gelu_both(v)
        H[j, 4 * m[0] + 2 * m[1] + m[2], p] = value.astype(BF)
        ACa[j, p, base, last] = slope
        double_first(0, j, p, H)

    def make_grad(j, p):
        m = [bits[d] for d in order(j, p)]
        v, base, last = whole(1, j, p)
        G[j, 4 * m[0] + 2 * m[1] + m[2], p] = (v * ACa[j, p, base, last]).astype(BF)
        double_first(1, j, p, G)

    halve_first(0, 0, yh)
    gather_third(TA, tc, far)
    halve_first(0, 1, yh)
    gather_third(CA, cc, far)
    halve_first(0, 2, yh)
    gather_cross(CA, cc, yh, "0")
    halve_first(0, 3, yh)
    gather_second(TA, tc, far, "1")
    so_own.wait()
    mask_out_half(core, MO.at[core], WO.at[core])
    wo_c.wait_recv()
    crossed(cc, "0")
    halve_first(1, 0, yh)
    gather_second(CA, cc, far, "1")
    halve_first(1, 1, yh)
    gather_cross(TA, tc, far, "1")
    halve_first(1, 2, yh)
    halve_first(1, 3, yh)
    mi_c = push(MIS, MI.at[core], at_core)
    mo_c = push(MOS, MO.at[core], at_core)
    crossed(tc, "1")
    halve_first(0, 0, far)
    gather_cross(CA, cc, far, "1")
    for j in range(1, CHUNKS):
        halve_first(0, j, far)
    crossed(cc, "1")
    for j in range(CHUNKS):
        halve_first(1, j, far)
    for u in units:
        halve_second(0, *u)
    for u in units:
        halve_third(0, *u)
    for u in units:
        halve_second(1, *u)
    for u in parted:
        make_hidden(*u)
    for u in units:
        halve_third(1, *u)
    for u in parted:
        double_second(0, *u, H)
    for u in parted:
        make_grad(*u)
    for u in parted:
        double_third(0, *u, H)
    for u in parted:
        double_second(1, *u, G)

    every = slice(None)

    def out_part(A, p, k, weight, right_dim):
        left = jnp.concatenate([A[i, :, p].reshape(256, WIDE) for i in range(CHUNKS)], axis=1)
        R[k, p] = dot(left, weight[k], 1, right_dim).reshape(2, 2, 2, 2, 16, 512)

    def row_cross(n, p):
        return push(R.at[other, p], RX.at[n, p], at_core)

    def full(n, p, idx):
        return R[(core, p) + idx] + RX[(n, p) + idx]

    def row_first(cross, n, p):
        cross.wait_recv()
        T1[n, p, 0] = full(n, p, (1 - xb, every, every, 0)).astype(BF)
        a = push(T1.at[n, p, 0], U1.at[n, p, 0], at_xb)
        T1[n, p, 1] = full(n, p, (every, 1 - xa, every, 1)).astype(BF)
        b = push(T1.at[n, p, 1], U1.at[n, p, 1], at_xa)
        return a, b

    def row_second(copies, n, p):
        copies[0].wait_recv()
        T2[n, p, 0] = (full(n, p, (xb, 1 - xa, every, 0)) + U1[n, p, 0, 1 - xa].astype(F32)).astype(BF)
        a = push(T2.at[n, p, 0], U2.at[n, p, 0], at_xa)
        copies[1].wait_recv()
        T2[n, p, 1] = (full(n, p, (1 - xb, xa, every, 1)) + U1[n, p, 1, 1 - xb].astype(F32)).astype(BF)
        b = push(T2.at[n, p, 1], U2.at[n, p, 1], at_xb)
        return a, b

    def row_third(copies, n, p):
        def row_sum(v, hf):
            near = (xa, xb)[hf]
            return (
                full(n, p, (xb, xa, v, hf))
                + U1[n, p, hf, near, v].astype(F32)
                + U2[n, p, hf, v].astype(F32)
            )

        for hf in range(2):
            copies[hf].wait_recv()
            T3[n, p, hf] = row_sum(1 - yh, hf).astype(BF)
            KEEP[n, p, hf] = row_sum(yh, hf)

    def row_fourth(n, p):
        return push(T3.at[n, p], U3.at[n, p], at_yh)

    def row_last(copy, n, p, out):
        copy.wait_recv()
        out[p] = (KEEP[n, p] + U3[n, p].astype(F32)).astype(BF)

    def out_grad(k, to):
        def step(t, carry):
            j, c = lax.div(t, 2), pl.multiple_of(256 * lax.rem(t, 2), 256)
            left = H[j, :, :, :, pl.ds(c, 256)].reshape(768, 256)
            got = dot(left, CA[k].reshape(768, 512), 0, 0).reshape(2, 8, 16, 512)
            m = MO[k, pl.ds(2 * t, 2)].astype(F32)
            to(t, (got * m[:, None]).reshape(256, 512).astype(BF))
            return carry
        lax.fori_loop(0, 8, step, 0)

    def far_out(t, v):
        FO[pl.ds(pl.multiple_of(t * 256, 256), 256), :] = v

    def own_out(t, v):
        DO[pl.ds(pl.multiple_of(core * 2048 + t * 256, 256), 256), :] = v

    def in_grad(lo, hi, k, to):
        def step(i, carry):
            d = pl.multiple_of(i * 256, 256)
            left = TA[k, :, :, :, :, :, pl.ds(d, 256)].reshape(768, 256)
            for j in range(CHUNKS):
                got = dot(left, G[j].reshape(768, WIDE), 0, 0).reshape(2, 8, 16, WIDE)
                m = MI[k, pl.ds(2 * i, 2), :, WIDE * j : WIDE * (j + 1)].astype(F32)
                to(d, j, (got * m[:, None]).reshape(256, WIDE).astype(BF))
            return carry
        lax.fori_loop(lo, hi, step, 0)

    def far_in(d, j, v):
        FI[pl.ds(d, 256), WIDE * j : WIDE * (j + 1)] = v

    def own_in(d, j, v):
        DI[pl.ds(d, 256), pl.ds(pl.multiple_of(core * 2048 + WIDE * j, WIDE), WIDE)] = v

    def arrived(s, p):
        for j in range(CHUNKS):
            d3[s][j, p].wait_recv()

    cross0, cross1, pair0, pair1 = {}, {}, {}, {}

    def third_of(p):
        for j in range(CHUNKS):
            double_third(1, j, p, G)

    for p in range(PARTS):
        arrived(0, p)
        out_part(H, p, other, WO, 0)
        cross0[p] = row_cross(0, p)
        if p == 2:
            third_of(0)
        out_part(H, p, core, WO, 0)
    third_of(1)
    pair0[0] = row_first(cross0[0], 0, 0)
    third_of(2)
    for p in (1, 2):
        pair0[p] = row_first(cross0[p], 0, p)
    wo_c.wait_send()
    mo_c.wait_recv()
    out_grad(other, far_out)
    dwo_far = push(FO, DO.at[cols(core)], at_core)
    for p in range(PARTS):
        pair0[p] = row_second(pair0[p], 0, p)
    out_grad(core, own_out)
    for p in range(PARTS):
        row_third(pair0[p], 0, p)
        cross0[p].wait_send()

    def row_part(p):
        arrived(1, p)
        out_part(G, p, other, WI, 1)
        cross1[p] = row_cross(1, p)

    row_part(0)
    out_part(G, 0, core, WI, 1)
    row_part(1)
    pair1[0] = row_first(cross1[0], 1, 0)
    out_part(G, 1, core, WI, 1)
    row_part(2)
    last0 = [row_fourth(0, p) for p in range(PARTS)]
    pair1[1] = row_first(cross1[1], 1, 1)
    out_part(G, 2, core, WI, 1)
    pair1[0] = row_second(pair1[0], 1, 0)
    pair1[2] = row_first(cross1[2], 1, 2)
    wi_c.wait_send()
    mi_c.wait_recv()
    in_grad(0, 1, other, far_in)
    pair1[1] = row_second(pair1[1], 1, 1)
    row_third(pair1[0], 1, 0)
    last1 = [row_fourth(1, 0)]
    pair1[2] = row_second(pair1[2], 1, 2)
    in_grad(1, 2, other, far_in)
    dwi_far = push(FI, DI.at[:, cols(core)], at_core)
    row_third(pair1[1], 1, 1)
    last1.append(row_fourth(1, 1))
    row_third(pair1[2], 1, 2)
    last1.append(row_fourth(1, 2))
    in_grad(0, 2, core, own_in)
    for p in range(PARTS):
        row_last(last0[p], 0, p, res_o)
    for p in range(PARTS):
        row_last(last1[p], 1, p, tg_o)
    dwo_far.wait_recv()
    dwi_far.wait_recv()
    waited = [wo_c, wi_c] + list(cross0.values())
    for c in sent:
        if not any(c is w for w in waited):
            c.wait_send()


def leave(a, b, c, d, a_o, b_o, c_o, d_o, sem):
    pairs = []
    for i in range(4):
        pairs.append((c.at[pl.ds(128 * i, 128)], c_o.at[pl.ds(128 * i, 128)]))
        pairs.append((d.at[pl.ds(1024 * i, 1024)], d_o.at[pl.ds(1024 * i, 1024)]))
    pairs += [(a, a_o), (b, b_o)]
    copies = [pltpu.make_async_copy(src, dst, sem.at[k]) for k, (src, dst) in enumerate(pairs)]
    for copy in copies:
        copy.start()
    for copy in copies:
        copy.wait()


def body(tokens, weight_in, mask_in, weight_out, mask_out, cotangent):
    anywhere = pl.BlockSpec(memory_space=pl.ANY)
    vmem = pl.BlockSpec(memory_space=pltpu.VMEM)
    smem = pl.BlockSpec(memory_space=pltpu.SMEM)

    def halving():
        return [
            pltpu.VMEM((CHUNKS, PARTS, 2, 2, 32, WIDE), BF),
            pltpu.VMEM((CHUNKS, PARTS, 2, 2, 32, WIDE), BF),
            pltpu.VMEM((CHUNKS, PARTS, 2, 2, 32, WIDE), F32),
            pltpu.VMEM((CHUNKS, PARTS, 2, 32, WIDE), BF),
            pltpu.VMEM((CHUNKS, PARTS, 2, 32, WIDE), BF),
            pltpu.VMEM((CHUNKS, PARTS, 32, WIDE), BF),
            pltpu.VMEM((CHUNKS, PARTS, 32, WIDE), BF),
        ]

    held = pl.pallas_call(
        kernel,
        out_shape=(
            OUT_KIND((PARTS, 2, 16, 512), BF),
            OUT_KIND((PARTS, 2, 16, 512), BF),
            OUT_KIND((512, 4096), BF),
            OUT_KIND((4096, 512), BF),
        ),
        in_specs=[anywhere] * 4 + [smem] * 2,
        out_specs=(vmem,) * 4,
        scratch_shapes=[
            pltpu.VMEM((2, 2, 2, 2, 2, 48, 512), BF),
            pltpu.VMEM((2, 2, 2, 2, 2, 48, 512), BF),
            pltpu.VMEM((2, 512, 2048), BF),
            pltpu.VMEM((2, 2048, 512), BF),
            pltpu.VMEM((512, 2048), BF),
            pltpu.VMEM((2048, 512), BF),
            pltpu.VMEM((4, 16, 2048), BF),
            pltpu.VMEM((2, 4, 16, 2048), BF),
            pltpu.VMEM((16, 16, 512), BF),
            pltpu.VMEM((2, 16, 16, 512), BF),
        ]
        + halving()
        + halving()
        + [
            pltpu.VMEM((CHUNKS, 8, PARTS, 32, WIDE), BF),
            pltpu.VMEM((CHUNKS, 8, PARTS, 32, WIDE), BF),
            pltpu.VMEM((2, PARTS, 2, 2, 2, 2, 16, 512), F32),
            pltpu.VMEM((2, PARTS, 2, 2, 2, 2, 16, 512), F32),
            pltpu.VMEM((2, PARTS, 2, 2, 2, 16, 512), BF),
            pltpu.VMEM((2, PARTS, 2, 2, 2, 16, 512), BF),
            pltpu.VMEM((2, PARTS, 2, 2, 16, 512), BF),
            pltpu.VMEM((2, PARTS, 2, 2, 16, 512), BF),
            pltpu.VMEM((2, PARTS, 2, 16, 512), BF),
            pltpu.VMEM((2, PARTS, 2, 16, 512), BF),
            pltpu.VMEM((2, PARTS, 2, 16, 512), F32),
            pltpu.SemaphoreType.DMA((N_COPIES,)),
            pltpu.SemaphoreType.DMA((N_COPIES,)),
            pltpu.SemaphoreType.DMA((8,)),
        ],
        compiler_params=pltpu.CompilerParams(
            collective_id=0, has_side_effects=True, vmem_limit_bytes=VMEM_BYTES
        ),
    )(tokens.reshape(2, 48, 512), cotangent.reshape(2, 48, 512), weight_in, weight_out, mask_in, mask_out.T)
    shapes = ((PARTS, 2, 16, 512), (PARTS, 2, 16, 512), (512, 4096), (4096, 512))
    result, tokens_grad, dwi, dwo = pl.pallas_call(
        leave,
        out_shape=tuple(jax.ShapeDtypeStruct(shape, BF) for shape in shapes),
        in_specs=[anywhere] * 4,
        out_specs=(anywhere,) * 4,
        scratch_shapes=[pltpu.SemaphoreType.DMA((10,))],
        compiler_params=pltpu.CompilerParams(vmem_limit_bytes=1024 * 1024),
    )(*held)
    return result.reshape(96, 512), tokens_grad.reshape(96, 512), dwi, dwo


def solution(mesh):
    return jax.shard_map(
        body,
        mesh=mesh,
        in_specs=(
            P("row", "col"),
            P("col", "row"),
            P("col", "row"),
            P("row", "col"),
            P("row", "col"),
            P("row", "col"),
        ),
        out_specs=(P("row", "col"), P("row", "col"), P("col", "row"), P("row", "col")),
        check_vma=False,
    )
```

```python
import jax
import jax.numpy as jnp
from jax import lax
from jax.experimental import pallas as pl
from jax.experimental.pallas import tpu as pltpu
from jax.sharding import PartitionSpec as P

BLOCK = 128
CHUNKS = 4
WIDE = 512
BF = jnp.bfloat16
F32 = jnp.float32

root_two_pi = 0.7978845608
cubic_coef = 0.044715

ORDERS = ((0, 1, 2), (1, 2, 0), (2, 0, 1))
PARTS = 3


def order(j, p):
    return ORDERS[(j + p) % 3]


def dot(left, right, left_dim, right_dim):
    return lax.dot_general(
        left, right, (((left_dim,), (right_dim,)), ((), ())), preferred_element_type=F32
    )


def gelu_both(values):
    tangent = jnp.tanh(root_two_pi * (values + cubic_coef * values * values * values))
    value = 0.5 * values * (1.0 + tangent)
    slope = 0.5 * (1.0 + tangent) + 0.5 * values * (1.0 - tangent * tangent) * root_two_pi * (
        1.0 + 3.0 * cubic_coef * values * values
    )
    return value, slope
OUT_KIND = pltpu.VMEM
VMEM_BYTES = 53 * 1024 * 1024


N_COPIES = 288


def kernel(
    tok, cot, win, wout, mask_in, mask_out_t,
    res_o, tg_o, DI, DO,
    TA, CA, WI, WO, FI, FO, MIS, MI, MOS, MO,
    S1a, R1a, ACa, S2a, R2a, S3a, R3a,
    S1b, R1b, ACb, S2b, R2b, S3b, R3b,
    H, G, R, RX, T1, U1, T2, U2, KEEP,
    send_sem, recv_sem, local_sem,
):
    row = lax.axis_index("row")
    col = lax.axis_index("col")
    x, yh = lax.div(row, 2), lax.rem(row, 2)
    yl = lax.div(col, 8)
    z = lax.div(lax.rem(col, 8), 2)
    core = lax.rem(col, 2)
    other = 1 - core
    xb, xa = lax.div(x, 2), lax.rem(lax.div(x + 1, 2), 2)
    zb, za = lax.div(z, 2), lax.rem(lax.div(z + 1, 2), 2)
    at_core = {"row": row, "col": col + 1 - 2 * core}
    at_y = {"row": row, "col": col + 8 - 16 * yl}
    at_za = {"row": row, "col": col + 2 * (1 - 2 * lax.rem(z, 2))}
    at_zb = {"row": row, "col": col + 2 * (3 - 2 * z)}
    at_xa = {"row": row + 2 * (1 - 2 * lax.rem(x, 2)), "col": col}
    at_xb = {"row": row + 2 * (3 - 2 * x), "col": col}
    at_yh = {"row": row + 1 - 2 * yh, "col": col}
    at_xa_yh = {"row": at_xa["row"] + 1 - 2 * yh, "col": col}
    at_xb_yh = {"row": at_xb["row"] + 1 - 2 * yh, "col": col}
    bits = (yl, za, zb)
    partner = (at_y, at_za, at_zb)

    count = [0]
    sent = []

    def push(src, dst, where):
        k = count[0]
        count[0] += 1
        copy = pltpu.make_async_remote_copy(
            src_ref=src, dst_ref=dst, send_sem=send_sem.at[k], recv_sem=recv_sem.at[k],
            device_id=where, device_id_type=pl.DeviceIdType.MESH,
        )
        copy.start()
        sent.append(copy)
        return copy

    lcount = [0]

    def local(src, dst):
        k = lcount[0]
        lcount[0] += 1
        copy = pltpu.make_async_copy(src, dst, local_sem.at[k])
        copy.start()
        return copy

    def cols(h):
        return pl.ds(pl.multiple_of(h * 2048, 2048), 2048)

    barrier = pltpu.get_barrier_semaphore()
    for where in (at_core, at_y, at_za, at_zb, at_xa, at_xb, at_yh, at_xa_yh, at_xb_yh):
        pl.semaphore_signal(barrier, inc=1, device_id=where, device_id_type=pl.DeviceIdType.MESH)

    tok_in = local(tok, TA.at[core, xb, xa, yh])
    cot_in = local(cot, CA.at[core, xb, xa, yh])
    si_far = local(win.at[:, cols(other)], DI.at[:, cols(other)])
    si_own = local(win.at[:, cols(core)], DI.at[:, cols(core)])
    so_far = local(wout.at[cols(other)], DO.at[cols(other)])
    so_own = local(wout.at[cols(core)], DO.at[cols(core)])

    def spread(scalar):
        return jnp.full((16, BLOCK), scalar.astype(F32), F32).astype(BF)

    def expand_in(h, dst):
        def step(j, carry):
            for i in range(4):
                dst[i, :, pl.ds(pl.multiple_of(j * BLOCK, BLOCK), BLOCK)] = spread(
                    mask_in[i, h * 16 + j]
                )
            return carry
        lax.fori_loop(0, 16, step, 0)

    def expand_out(h, dst):
        def step(i, carry):
            for j in range(4):
                dst[i, :, BLOCK * j : BLOCK * (j + 1)] = spread(mask_out_t[j, h * 16 + i])
            return carry
        lax.fori_loop(0, 16, step, 0)

    expand_in(other, MIS)
    expand_in(core, MI.at[core])
    expand_out(other, MOS)
    expand_out(core, MO.at[core])
    pl.semaphore_wait(barrier, 9)

    def gather_y(A, c):
        for hf in range(2):
            at = A.at[core, xb, xa, yh, hf]
            c["y%d" % hf] = push(at, at, at_yh)

    def gather_first(A, c):
        c["a0"] = push(A.at[core, xb, xa, yh, 0], A.at[core, xb, xa, yh, 0], at_xb)
        c["b0"] = push(A.at[core, xb, xa, yh, 1], A.at[core, xb, xa, yh, 1], at_xa)

    def gather_second(A, c, v, tag):
        c["a" + tag].wait_recv()
        c["A" + tag] = push(A.at[core, :, xa, v, 0], A.at[core, :, xa, v, 0], at_xa)
        c["b" + tag].wait_recv()
        c["B" + tag] = push(A.at[core, xb, :, v, 1], A.at[core, xb, :, v, 1], at_xb)

    def gather_third(A, c, v):
        c["y0"].wait_recv()
        c["a1"] = push(A.at[core, xb, xa, v, 0], A.at[core, xb, xa, v, 0], at_xb)
        c["y1"].wait_recv()
        c["b1"] = push(A.at[core, xb, xa, v, 1], A.at[core, xb, xa, v, 1], at_xa)

    def gather_cross(A, c, v, tag):
        c["A" + tag].wait_recv()
        one = push(A.at[core, :, :, v, 0], A.at[core, :, :, v, 0], at_core)
        c["B" + tag].wait_recv()
        two = push(A.at[core, :, :, v, 1], A.at[core, :, :, v, 1], at_core)
        c["c" + tag] = (one, two)

    def crossed(c, tag):
        for copy in c["c" + tag]:
            copy.wait_recv()

    def mask_in_half(h, m, dst):
        def step(i, carry):
            r = pl.multiple_of(i * BLOCK, BLOCK)
            w = DI[pl.ds(r, BLOCK), cols(h)].reshape(8, 16, 2048)
            dst[pl.ds(r, BLOCK), :] = (w * m[i][None]).reshape(BLOCK, 2048)
            return carry
        lax.fori_loop(0, 4, step, 0)

    def mask_out_half(h, m, dst):
        def step(i, carry):
            r = pl.multiple_of(i * BLOCK, BLOCK)
            w = DO[pl.ds(pl.multiple_of(h * 2048 + r, BLOCK), BLOCK), :].reshape(8, 16, 512)
            dst[pl.ds(r, BLOCK), :] = (w * m[i][None]).reshape(BLOCK, 512)
            return carry
        lax.fori_loop(0, 16, step, 0)

    far = 1 - yh
    tok_in.wait()
    tc, cc = {}, {}
    gather_y(TA, tc)
    gather_first(TA, tc)
    cot_in.wait()
    gather_y(CA, cc)
    si_far.wait()
    mask_in_half(other, MIS, FI)
    wi_c = push(FI, WI.at[core], at_core)
    gather_second(TA, tc, yh, "0")
    gather_first(CA, cc)
    si_own.wait()
    mask_in_half(core, MI.at[core], WI.at[core])
    gather_cross(TA, tc, yh, "0")
    gather_second(CA, cc, yh, "0")
    so_far.wait()
    mask_out_half(other, MOS, FO)
    wo_c = push(FO, WO.at[core], at_core)
    wi_c.wait_recv()
    crossed(tc, "0")

    def part_in(j, v):
        out = None
        for k in range(2):
            t = dot(TA[k, :, :, v].reshape(384, 512), WI[k, :, WIDE * j : WIDE * (j + 1)], 1, 0)
            out = t if out is None else out + t
        return out.reshape(2, 2, PARTS, 32, WIDE)

    def part_out(j, v):
        out = None
        for k in range(2):
            t = dot(CA[k, :, :, v].reshape(384, 512), WO[k, WIDE * j : WIDE * (j + 1), :], 1, 1)
            out = t if out is None else out + t
        return out.reshape(2, 2, PARTS, 32, WIDE)

    streams = ((part_in, S1a, R1a, ACa, S2a, R2a, S3a, R3a), (part_out, S1b, R1b, ACb, S2b, R2b, S3b, R3b))
    units = [(j, p) for j in range(CHUNKS) for p in range(PARTS)]
    parted = [(j, p) for p in range(PARTS) for j in range(CHUNKS)]
    first = [{u: () for u in units} for _ in range(2)]
    second, third = [{}, {}], [{}, {}]

    def halve_first(s, j, v):
        part, S1, R1, AC, S2, R2, S3, R3 = streams[s]
        got = part(j, v)
        for p in range(PARTS):
            d = order(j, p)[0]
            low = bits[d] == 0
            S1[j, p, :, v] = jnp.where(low, got[1, :, p], got[0, :, p]).astype(BF)
            c = push(S1.at[j, p, :, v], R1.at[j, p, :, v], partner[d])
            first[s][j, p] += (c,)
        for p in range(PARTS):
            low = bits[order(j, p)[0]] == 0
            AC[j, p, :, v] = jnp.where(low, got[0, :, p], got[1, :, p])

    def halve_second(s, j, p):
        part, S1, R1, AC, S2, R2, S3, R3 = streams[s]
        d = order(j, p)[1]
        away, keep = 1 - bits[d], bits[d]
        for c in first[s][j, p]:
            c.wait_recv()
        S2[j, p] = (AC[j, p, away] + R1[j, p, away].astype(F32)).astype(BF)
        second[s][j, p] = push(S2.at[j, p], R2.at[j, p], partner[d])
        AC[j, p, keep] = AC[j, p, keep] + R1[j, p, keep].astype(F32)

    def halve_third(s, j, p):
        part, S1, R1, AC, S2, R2, S3, R3 = streams[s]
        base, d = bits[order(j, p)[1]], order(j, p)[2]
        away, keep = 1 - bits[d], bits[d]
        second[s][j, p].wait_recv()
        S3[j, p] = (AC[j, p, base, away] + R2[j, p, away].astype(F32)).astype(BF)
        third[s][j, p] = push(S3.at[j, p], R3.at[j, p], partner[d])
        AC[j, p, base, keep] = AC[j, p, base, keep] + R2[j, p, keep].astype(F32)

    def whole(s, j, p):
        part, S1, R1, AC, S2, R2, S3, R3 = streams[s]
        third[s][j, p].wait_recv()
        base, last = bits[order(j, p)[1]], bits[order(j, p)[2]]
        return AC[j, p, base, last] + R3[j, p].astype(F32), base, last

    d1, d2, d3 = [{}, {}], [{}, {}], [{}, {}]

    def double_first(s, j, p, A):
        m = [bits[d] for d in order(j, p)]
        at = A.at[j, 4 * m[0] + 2 * m[1] + m[2], p]
        d1[s][j, p] = push(at, at, partner[order(j, p)[2]])

    def double_second(s, j, p, A):
        m = [bits[d] for d in order(j, p)]
        d1[s][j, p].wait_recv()
        at = A.at[j, pl.ds(4 * m[0] + 2 * m[1], 2), p]
        d2[s][j, p] = push(at, at, partner[order(j, p)[1]])

    def double_third(s, j, p, A):
        m = [bits[d] for d in order(j, p)]
        d2[s][j, p].wait_recv()
        at = A.at[j, pl.ds(4 * m[0], 4), p]
        d3[s][j, p] = push(at, at, partner[order(j, p)[0]])

    def make_hidden(j, p):
        m = [bits[d] for d in order(j, p)]
        v, base, last = whole(0, j, p)
        value, slope = gelu_both(v)
        H[j, 4 * m[0] + 2 * m[1] + m[2], p] = value.astype(BF)
        ACa[j, p, base, last] = slope
        double_first(0, j, p, H)

    def make_grad(j, p):
        m = [bits[d] for d in order(j, p)]
        v, base, last = whole(1, j, p)
        G[j, 4 * m[0] + 2 * m[1] + m[2], p] = (v * ACa[j, p, base, last]).astype(BF)
        double_first(1, j, p, G)

    halve_first(0, 0, yh)
    gather_third(TA, tc, far)
    halve_first(0, 1, yh)
    gather_third(CA, cc, far)
    halve_first(0, 2, yh)
    gather_cross(CA, cc, yh, "0")
    halve_first(0, 3, yh)
    gather_second(TA, tc, far, "1")
    so_own.wait()
    mask_out_half(core, MO.at[core], WO.at[core])
    wo_c.wait_recv()
    crossed(cc, "0")
    halve_first(1, 0, yh)
    gather_second(CA, cc, far, "1")
    halve_first(1, 1, yh)
    gather_cross(TA, tc, far, "1")
    halve_first(1, 2, yh)
    halve_first(1, 3, yh)
    mi_c = push(MIS, MI.at[core], at_core)
    mo_c = push(MOS, MO.at[core], at_core)
    crossed(tc, "1")
    halve_first(0, 0, far)
    gather_cross(CA, cc, far, "1")
    for j in range(1, CHUNKS):
        halve_first(0, j, far)
    crossed(cc, "1")
    for j in range(CHUNKS):
        halve_first(1, j, far)
    for u in units:
        halve_second(0, *u)
    for u in units:
        halve_third(0, *u)
    for u in units:
        halve_second(1, *u)
    for u in parted:
        make_hidden(*u)
    for u in units:
        halve_third(1, *u)
    for u in parted:
        double_second(0, *u, H)
    for u in parted:
        make_grad(*u)
    for u in parted:
        double_third(0, *u, H)
    for u in parted:
        double_second(1, *u, G)

    every = slice(None)

    def out_part(A, p, k, weight, right_dim):
        left = jnp.concatenate([A[i, :, p].reshape(256, WIDE) for i in range(CHUNKS)], axis=1)
        R[k, p] = dot(left, weight[k], 1, right_dim).reshape(2, 2, 2, 2, 16, 512)

    def row_cross(n, p):
        return push(R.at[other, p], RX.at[n, p], at_core)

    def full(n, p, idx):
        return R[(core, p) + idx] + RX[(n, p) + idx]

    def row_first(cross, n, p):
        cross.wait_recv()
        T1[n, p, 0] = full(n, p, (1 - xb, every, every, 0)).astype(BF)
        a = push(T1.at[n, p, 0], U1.at[n, p, 0], at_xb)
        T1[n, p, 1] = full(n, p, (every, 1 - xa, every, 1)).astype(BF)
        b = push(T1.at[n, p, 1], U1.at[n, p, 1], at_xa)
        return a, b

    def row_second(copies, n, p):
        copies[0].wait_recv()
        T2[n, p, 0] = (full(n, p, (xb, every, every, 0)) + U1[n, p, 0].astype(F32)).astype(BF)
        KEEP[n, p, 0] = full(n, p, (xb, xa, yh, 0)) + U1[n, p, 0, xa, yh].astype(F32)
        copies[1].wait_recv()
        T2[n, p, 1] = (full(n, p, (every, xa, every, 1)) + U1[n, p, 1].astype(F32)).astype(BF)
        KEEP[n, p, 1] = full(n, p, (xb, xa, yh, 1)) + U1[n, p, 1, xb, yh].astype(F32)

    def row_direct(n, p):
        got = []
        for hf, mine, side, corner in ((0, xa, at_xa, at_xa_yh), (1, xb, at_xb, at_xb_yh)):
            got.append(push(T2.at[n, p, hf, 1 - mine, 1 - yh], U2.at[n, p, hf, 0], corner))
            got.append(push(T2.at[n, p, hf, mine, 1 - yh], U2.at[n, p, hf, 1], at_yh))
            got.append(push(T2.at[n, p, hf, 1 - mine, yh], U2.at[n, p, hf, 2], side))
        return got

    def row_last(copies, n, p, out):
        for copy in copies:
            copy.wait_recv()
        total = KEEP[n, p]
        for k in range(3):
            total = total + U2[n, p, :, k].astype(F32)
        out[p] = total.astype(BF)

    def out_grad(k, to):
        def step(t, carry):
            j, c = lax.div(t, 2), pl.multiple_of(256 * lax.rem(t, 2), 256)
            left = H[j, :, :, :, pl.ds(c, 256)].reshape(768, 256)
            got = dot(left, CA[k].reshape(768, 512), 0, 0).reshape(2, 8, 16, 512)
            m = MO[k, pl.ds(2 * t, 2)].astype(F32)
            to(t, (got * m[:, None]).reshape(256, 512).astype(BF))
            return carry
        lax.fori_loop(0, 8, step, 0)

    def far_out(t, v):
        FO[pl.ds(pl.multiple_of(t * 256, 256), 256), :] = v

    def own_out(t, v):
        DO[pl.ds(pl.multiple_of(core * 2048 + t * 256, 256), 256), :] = v

    def in_grad(lo, hi, k, to):
        def step(i, carry):
            d = pl.multiple_of(i * 256, 256)
            left = TA[k, :, :, :, :, :, pl.ds(d, 256)].reshape(768, 256)
            for j in range(CHUNKS):
                got = dot(left, G[j].reshape(768, WIDE), 0, 0).reshape(2, 8, 16, WIDE)
                m = MI[k, pl.ds(2 * i, 2), :, WIDE * j : WIDE * (j + 1)].astype(F32)
                to(d, j, (got * m[:, None]).reshape(256, WIDE).astype(BF))
            return carry
        lax.fori_loop(lo, hi, step, 0)

    def far_in(d, j, v):
        FI[pl.ds(d, 256), WIDE * j : WIDE * (j + 1)] = v

    def own_in(d, j, v):
        DI[pl.ds(d, 256), pl.ds(pl.multiple_of(core * 2048 + WIDE * j, WIDE), WIDE)] = v

    def arrived(s, p):
        for j in range(CHUNKS):
            d3[s][j, p].wait_recv()

    cross0, cross1, pair0, pair1 = {}, {}, {}, {}

    def third_of(p):
        for j in range(CHUNKS):
            double_third(1, j, p, G)

    for p in range(PARTS):
        arrived(0, p)
        out_part(H, p, other, WO, 0)
        cross0[p] = row_cross(0, p)
        if p == 2:
            third_of(0)
        out_part(H, p, core, WO, 0)
    third_of(1)
    pair0[0] = row_first(cross0[0], 0, 0)
    third_of(2)
    for p in (1, 2):
        pair0[p] = row_first(cross0[p], 0, p)
    wo_c.wait_send()
    mo_c.wait_recv()
    out_grad(other, far_out)
    dwo_far = push(FO, DO.at[cols(core)], at_core)
    for p in range(PARTS):
        row_second(pair0[p], 0, p)
        cross0[p].wait_send()
    out_grad(core, own_out)

    def row_part(p):
        arrived(1, p)
        out_part(G, p, other, WI, 1)
        cross1[p] = row_cross(1, p)

    row_part(0)
    out_part(G, 0, core, WI, 1)
    row_part(1)
    pair1[0] = row_first(cross1[0], 1, 0)
    out_part(G, 1, core, WI, 1)
    row_part(2)
    last0 = [row_direct(0, p) for p in range(PARTS)]
    pair1[1] = row_first(cross1[1], 1, 1)
    out_part(G, 2, core, WI, 1)
    last1 = []
    row_second(pair1[0], 1, 0)
    last1.append(row_direct(1, 0))
    pair1[2] = row_first(cross1[2], 1, 2)
    wi_c.wait_send()
    mi_c.wait_recv()
    in_grad(0, 1, other, far_in)
    row_second(pair1[1], 1, 1)
    last1.append(row_direct(1, 1))
    in_grad(1, 2, other, far_in)
    dwi_far = push(FI, DI.at[:, cols(core)], at_core)
    row_second(pair1[2], 1, 2)
    last1.append(row_direct(1, 2))
    in_grad(0, 2, core, own_in)
    for p in range(PARTS):
        row_last(last0[p], 0, p, res_o)
    for p in range(PARTS):
        row_last(last1[p], 1, p, tg_o)
    dwo_far.wait_recv()
    dwi_far.wait_recv()
    waited = [wo_c, wi_c] + list(cross0.values())
    for c in sent:
        if not any(c is w for w in waited):
            c.wait_send()


def leave(a, b, c, d, a_o, b_o, c_o, d_o, sem):
    pairs = []
    for i in range(4):
        pairs.append((c.at[pl.ds(128 * i, 128)], c_o.at[pl.ds(128 * i, 128)]))
        pairs.append((d.at[pl.ds(1024 * i, 1024)], d_o.at[pl.ds(1024 * i, 1024)]))
    pairs += [(a, a_o), (b, b_o)]
    copies = [pltpu.make_async_copy(src, dst, sem.at[k]) for k, (src, dst) in enumerate(pairs)]
    for copy in copies:
        copy.start()
    for copy in copies:
        copy.wait()


def body(tokens, weight_in, mask_in, weight_out, mask_out, cotangent):
    anywhere = pl.BlockSpec(memory_space=pl.ANY)
    vmem = pl.BlockSpec(memory_space=pltpu.VMEM)
    smem = pl.BlockSpec(memory_space=pltpu.SMEM)

    def halving():
        return [
            pltpu.VMEM((CHUNKS, PARTS, 2, 2, 32, WIDE), BF),
            pltpu.VMEM((CHUNKS, PARTS, 2, 2, 32, WIDE), BF),
            pltpu.VMEM((CHUNKS, PARTS, 2, 2, 32, WIDE), F32),
            pltpu.VMEM((CHUNKS, PARTS, 2, 32, WIDE), BF),
            pltpu.VMEM((CHUNKS, PARTS, 2, 32, WIDE), BF),
            pltpu.VMEM((CHUNKS, PARTS, 32, WIDE), BF),
            pltpu.VMEM((CHUNKS, PARTS, 32, WIDE), BF),
        ]

    held = pl.pallas_call(
        kernel,
        out_shape=(
            OUT_KIND((PARTS, 2, 16, 512), BF),
            OUT_KIND((PARTS, 2, 16, 512), BF),
            OUT_KIND((512, 4096), BF),
            OUT_KIND((4096, 512), BF),
        ),
        in_specs=[anywhere] * 4 + [smem] * 2,
        out_specs=(vmem,) * 4,
        scratch_shapes=[
            pltpu.VMEM((2, 2, 2, 2, 2, 48, 512), BF),
            pltpu.VMEM((2, 2, 2, 2, 2, 48, 512), BF),
            pltpu.VMEM((2, 512, 2048), BF),
            pltpu.VMEM((2, 2048, 512), BF),
            pltpu.VMEM((512, 2048), BF),
            pltpu.VMEM((2048, 512), BF),
            pltpu.VMEM((4, 16, 2048), BF),
            pltpu.VMEM((2, 4, 16, 2048), BF),
            pltpu.VMEM((16, 16, 512), BF),
            pltpu.VMEM((2, 16, 16, 512), BF),
        ]
        + halving()
        + halving()
        + [
            pltpu.VMEM((CHUNKS, 8, PARTS, 32, WIDE), BF),
            pltpu.VMEM((CHUNKS, 8, PARTS, 32, WIDE), BF),
            pltpu.VMEM((2, PARTS, 2, 2, 2, 2, 16, 512), F32),
            pltpu.VMEM((2, PARTS, 2, 2, 2, 2, 16, 512), F32),
            pltpu.VMEM((2, PARTS, 2, 2, 2, 16, 512), BF),
            pltpu.VMEM((2, PARTS, 2, 2, 2, 16, 512), BF),
            pltpu.VMEM((2, PARTS, 2, 2, 2, 16, 512), BF),
            pltpu.VMEM((2, PARTS, 2, 3, 16, 512), BF),
            pltpu.VMEM((2, PARTS, 2, 16, 512), F32),
            pltpu.SemaphoreType.DMA((N_COPIES,)),
            pltpu.SemaphoreType.DMA((N_COPIES,)),
            pltpu.SemaphoreType.DMA((8,)),
        ],
        compiler_params=pltpu.CompilerParams(
            collective_id=0, has_side_effects=True, vmem_limit_bytes=VMEM_BYTES
        ),
    )(tokens.reshape(2, 48, 512), cotangent.reshape(2, 48, 512), weight_in, weight_out, mask_in, mask_out.T)
    shapes = ((PARTS, 2, 16, 512), (PARTS, 2, 16, 512), (512, 4096), (4096, 512))
    result, tokens_grad, dwi, dwo = pl.pallas_call(
        leave,
        out_shape=tuple(jax.ShapeDtypeStruct(shape, BF) for shape in shapes),
        in_specs=[anywhere] * 4,
        out_specs=(anywhere,) * 4,
        scratch_shapes=[pltpu.SemaphoreType.DMA((10,))],
        compiler_params=pltpu.CompilerParams(vmem_limit_bytes=1024 * 1024),
    )(*held)
    return result.reshape(96, 512), tokens_grad.reshape(96, 512), dwi, dwo


def solution(mesh):
    return jax.shard_map(
        body,
        mesh=mesh,
        in_specs=(
            P("row", "col"),
            P("col", "row"),
            P("col", "row"),
            P("row", "col"),
            P("row", "col"),
            P("row", "col"),
        ),
        out_specs=(P("row", "col"), P("row", "col"), P("col", "row"), P("row", "col")),
        check_vma=False,
    )
```

```python
import jax
import jax.numpy as jnp
from jax import lax
from jax.experimental import pallas as pl
from jax.experimental.pallas import tpu as pltpu
from jax.sharding import PartitionSpec as P

BLOCK = 128
CHUNKS = 4
WIDE = 512
BF = jnp.bfloat16
F32 = jnp.float32

root_two_pi = 0.7978845608
cubic_coef = 0.044715

ORDERS = ((0, 1, 2), (1, 2, 0), (2, 0, 1))
PARTS = 3


def order(j, p):
    return ORDERS[(j + p) % 3]


def dot(left, right, left_dim, right_dim):
    return lax.dot_general(
        left, right, (((left_dim,), (right_dim,)), ((), ())), preferred_element_type=F32
    )


def gelu_both(values):
    tangent = jnp.tanh(root_two_pi * (values + cubic_coef * values * values * values))
    value = 0.5 * values * (1.0 + tangent)
    slope = 0.5 * (1.0 + tangent) + 0.5 * values * (1.0 - tangent * tangent) * root_two_pi * (
        1.0 + 3.0 * cubic_coef * values * values
    )
    return value, slope
OUT_KIND = pltpu.VMEM
VMEM_BYTES = 53 * 1024 * 1024


N_COPIES = 288


def kernel(
    tok, cot, win, wout, mask_in, mask_out_t,
    res_o, tg_o, DI, DO,
    TA, CA, WI, WO, FI, FO, MIS, MI, MOS, MO,
    S1a, R1a, ACa, S2a, R2a, S3a, R3a,
    S1b, R1b, ACb, S2b, R2b, S3b, R3b,
    H, G, R, RX, T1, U1, T2, U2, KEEP,
    send_sem, recv_sem, local_sem,
):
    row = lax.axis_index("row")
    col = lax.axis_index("col")
    x, yh = lax.div(row, 2), lax.rem(row, 2)
    yl = lax.div(col, 8)
    z = lax.div(lax.rem(col, 8), 2)
    core = lax.rem(col, 2)
    other = 1 - core
    xb, xa = lax.div(x, 2), lax.rem(lax.div(x + 1, 2), 2)
    zb, za = lax.div(z, 2), lax.rem(lax.div(z + 1, 2), 2)
    at_core = {"row": row, "col": col + 1 - 2 * core}
    at_y = {"row": row, "col": col + 8 - 16 * yl}
    at_za = {"row": row, "col": col + 2 * (1 - 2 * lax.rem(z, 2))}
    at_zb = {"row": row, "col": col + 2 * (3 - 2 * z)}
    at_xa = {"row": row + 2 * (1 - 2 * lax.rem(x, 2)), "col": col}
    at_xb = {"row": row + 2 * (3 - 2 * x), "col": col}
    at_yh = {"row": row + 1 - 2 * yh, "col": col}
    at_xa_yh = {"row": at_xa["row"] + 1 - 2 * yh, "col": col}
    at_xb_yh = {"row": at_xb["row"] + 1 - 2 * yh, "col": col}
    bits = (yl, za, zb)
    partner = (at_y, at_za, at_zb)

    count = [0]
    sent = []

    def push(src, dst, where):
        k = count[0]
        count[0] += 1
        copy = pltpu.make_async_remote_copy(
            src_ref=src, dst_ref=dst, send_sem=send_sem.at[k], recv_sem=recv_sem.at[k],
            device_id=where, device_id_type=pl.DeviceIdType.MESH,
        )
        copy.start()
        sent.append(copy)
        return copy

    lcount = [0]

    def local(src, dst):
        k = lcount[0]
        lcount[0] += 1
        copy = pltpu.make_async_copy(src, dst, local_sem.at[k])
        copy.start()
        return copy

    def cols(h):
        return pl.ds(pl.multiple_of(h * 2048, 2048), 2048)

    barrier = pltpu.get_barrier_semaphore()
    for where in (at_core, at_y, at_za, at_zb, at_xa, at_xb, at_yh, at_xa_yh, at_xb_yh):
        pl.semaphore_signal(barrier, inc=1, device_id=where, device_id_type=pl.DeviceIdType.MESH)

    tok_in = local(tok, TA.at[core, xb, xa, yh])
    cot_in = local(cot, CA.at[core, xb, xa, yh])
    si_far = local(win.at[:, cols(other)], DI.at[:, cols(other)])
    si_own = local(win.at[:, cols(core)], DI.at[:, cols(core)])
    so_far = local(wout.at[cols(other)], DO.at[cols(other)])
    so_own = local(wout.at[cols(core)], DO.at[cols(core)])

    def spread(scalar):
        return jnp.full((16, BLOCK), scalar.astype(F32), F32).astype(BF)

    def expand_in(h, dst):
        def step(j, carry):
            for i in range(4):
                dst[i, :, pl.ds(pl.multiple_of(j * BLOCK, BLOCK), BLOCK)] = spread(
                    mask_in[i, h * 16 + j]
                )
            return carry
        lax.fori_loop(0, 16, step, 0)

    def expand_out(h, dst):
        def step(i, carry):
            for j in range(4):
                dst[i, :, BLOCK * j : BLOCK * (j + 1)] = spread(mask_out_t[j, h * 16 + i])
            return carry
        lax.fori_loop(0, 16, step, 0)

    expand_in(other, MIS)
    expand_in(core, MI.at[core])
    expand_out(other, MOS)
    expand_out(core, MO.at[core])
    pl.semaphore_wait(barrier, 9)

    def gather_y(A, c):
        for hf in range(2):
            at = A.at[core, xb, xa, yh, hf]
            c["y%d" % hf] = push(at, at, at_yh)

    def gather_first(A, c):
        c["a0"] = push(A.at[core, xb, xa, yh, 0], A.at[core, xb, xa, yh, 0], at_xb)
        c["b0"] = push(A.at[core, xb, xa, yh, 1], A.at[core, xb, xa, yh, 1], at_xa)

    def gather_second(A, c, v, tag):
        c["a" + tag].wait_recv()
        c["A" + tag] = push(A.at[core, :, xa, v, 0], A.at[core, :, xa, v, 0], at_xa)
        c["b" + tag].wait_recv()
        c["B" + tag] = push(A.at[core, xb, :, v, 1], A.at[core, xb, :, v, 1], at_xb)

    def gather_third(A, c, v):
        c["y0"].wait_recv()
        c["a1"] = push(A.at[core, xb, xa, v, 0], A.at[core, xb, xa, v, 0], at_xb)
        c["y1"].wait_recv()
        c["b1"] = push(A.at[core, xb, xa, v, 1], A.at[core, xb, xa, v, 1], at_xa)

    def gather_cross(A, c, v, tag):
        c["A" + tag].wait_recv()
        one = push(A.at[core, :, :, v, 0], A.at[core, :, :, v, 0], at_core)
        c["B" + tag].wait_recv()
        two = push(A.at[core, :, :, v, 1], A.at[core, :, :, v, 1], at_core)
        c["c" + tag] = (one, two)

    def crossed(c, tag):
        for copy in c["c" + tag]:
            copy.wait_recv()

    def mask_in_half(h, m, dst):
        def step(i, carry):
            r = pl.multiple_of(i * BLOCK, BLOCK)
            w = DI[pl.ds(r, BLOCK), cols(h)].reshape(8, 16, 2048)
            dst[pl.ds(r, BLOCK), :] = (w * m[i][None]).reshape(BLOCK, 2048)
            return carry
        lax.fori_loop(0, 4, step, 0)

    def mask_out_half(h, m, dst):
        def step(i, carry):
            r = pl.multiple_of(i * BLOCK, BLOCK)
            w = DO[pl.ds(pl.multiple_of(h * 2048 + r, BLOCK), BLOCK), :].reshape(8, 16, 512)
            dst[pl.ds(r, BLOCK), :] = (w * m[i][None]).reshape(BLOCK, 512)
            return carry
        lax.fori_loop(0, 16, step, 0)

    far = 1 - yh
    tok_in.wait()
    tc, cc = {}, {}
    gather_y(TA, tc)
    gather_first(TA, tc)
    cot_in.wait()
    gather_y(CA, cc)
    si_far.wait()
    mask_in_half(other, MIS, FI)
    wi_c = push(FI, WI.at[core], at_core)
    gather_second(TA, tc, yh, "0")
    gather_first(CA, cc)
    si_own.wait()
    mask_in_half(core, MI.at[core], WI.at[core])
    gather_cross(TA, tc, yh, "0")
    gather_second(CA, cc, yh, "0")
    so_far.wait()
    mask_out_half(other, MOS, FO)
    wo_c = push(FO, WO.at[core], at_core)
    wi_c.wait_recv()
    crossed(tc, "0")

    def part_in(j, v):
        out = None
        for k in range(2):
            t = dot(TA[k, :, :, v].reshape(384, 512), WI[k, :, WIDE * j : WIDE * (j + 1)], 1, 0)
            out = t if out is None else out + t
        return out.reshape(2, 2, PARTS, 32, WIDE)

    def part_out(j, v):
        out = None
        for k in range(2):
            t = dot(CA[k, :, :, v].reshape(384, 512), WO[k, WIDE * j : WIDE * (j + 1), :], 1, 1)
            out = t if out is None else out + t
        return out.reshape(2, 2, PARTS, 32, WIDE)

    streams = ((part_in, S1a, R1a, ACa, S2a, R2a, S3a, R3a), (part_out, S1b, R1b, ACb, S2b, R2b, S3b, R3b))
    units = [(j, p) for j in range(CHUNKS) for p in range(PARTS)]
    parted = [(j, p) for p in range(PARTS) for j in range(CHUNKS)]
    first = [{u: () for u in units} for _ in range(2)]
    second, third = [{}, {}], [{}, {}]

    def halve_first(s, j, v):
        part, S1, R1, AC, S2, R2, S3, R3 = streams[s]
        got = part(j, v)
        for p in range(PARTS):
            d = order(j, p)[0]
            low = bits[d] == 0
            S1[j, p, :, v] = jnp.where(low, got[1, :, p], got[0, :, p]).astype(BF)
            c = push(S1.at[j, p, :, v], R1.at[j, p, :, v], partner[d])
            first[s][j, p] += (c,)
        for p in range(PARTS):
            low = bits[order(j, p)[0]] == 0
            AC[j, p, :, v] = jnp.where(low, got[0, :, p], got[1, :, p])

    def halve_second(s, j, p):
        part, S1, R1, AC, S2, R2, S3, R3 = streams[s]
        d = order(j, p)[1]
        away, keep = 1 - bits[d], bits[d]
        for c in first[s][j, p]:
            c.wait_recv()
        S2[j, p] = (AC[j, p, away] + R1[j, p, away].astype(F32)).astype(BF)
        second[s][j, p] = push(S2.at[j, p], R2.at[j, p], partner[d])
        AC[j, p, keep] = AC[j, p, keep] + R1[j, p, keep].astype(F32)

    def halve_third(s, j, p):
        part, S1, R1, AC, S2, R2, S3, R3 = streams[s]
        base, d = bits[order(j, p)[1]], order(j, p)[2]
        away, keep = 1 - bits[d], bits[d]
        second[s][j, p].wait_recv()
        S3[j, p] = (AC[j, p, base, away] + R2[j, p, away].astype(F32)).astype(BF)
        third[s][j, p] = push(S3.at[j, p], R3.at[j, p], partner[d])
        AC[j, p, base, keep] = AC[j, p, base, keep] + R2[j, p, keep].astype(F32)

    def whole(s, j, p):
        part, S1, R1, AC, S2, R2, S3, R3 = streams[s]
        third[s][j, p].wait_recv()
        base, last = bits[order(j, p)[1]], bits[order(j, p)[2]]
        return AC[j, p, base, last] + R3[j, p].astype(F32), base, last

    d1, d2, d3 = [{}, {}], [{}, {}], [{}, {}]

    def double_first(s, j, p, A):
        m = [bits[d] for d in order(j, p)]
        at = A.at[j, 4 * m[0] + 2 * m[1] + m[2], p]
        d1[s][j, p] = push(at, at, partner[order(j, p)[2]])

    def double_second(s, j, p, A):
        m = [bits[d] for d in order(j, p)]
        d1[s][j, p].wait_recv()
        at = A.at[j, pl.ds(4 * m[0] + 2 * m[1], 2), p]
        d2[s][j, p] = push(at, at, partner[order(j, p)[1]])

    def double_third(s, j, p, A):
        m = [bits[d] for d in order(j, p)]
        d2[s][j, p].wait_recv()
        at = A.at[j, pl.ds(4 * m[0], 4), p]
        d3[s][j, p] = push(at, at, partner[order(j, p)[0]])

    def make_hidden(j, p):
        m = [bits[d] for d in order(j, p)]
        v, base, last = whole(0, j, p)
        value, slope = gelu_both(v)
        H[j, 4 * m[0] + 2 * m[1] + m[2], p] = value.astype(BF)
        ACa[j, p, base, last] = slope
        double_first(0, j, p, H)

    def make_grad(j, p):
        m = [bits[d] for d in order(j, p)]
        v, base, last = whole(1, j, p)
        G[j, 4 * m[0] + 2 * m[1] + m[2], p] = (v * ACa[j, p, base, last]).astype(BF)
        double_first(1, j, p, G)

    halve_first(0, 0, yh)
    gather_third(TA, tc, far)
    halve_first(0, 1, yh)
    gather_third(CA, cc, far)
    halve_first(0, 2, yh)
    gather_cross(CA, cc, yh, "0")
    halve_first(0, 3, yh)
    gather_second(TA, tc, far, "1")
    so_own.wait()
    mask_out_half(core, MO.at[core], WO.at[core])
    wo_c.wait_recv()
    crossed(cc, "0")
    halve_first(1, 0, yh)
    gather_second(CA, cc, far, "1")
    halve_first(1, 1, yh)
    gather_cross(TA, tc, far, "1")
    halve_first(1, 2, yh)
    halve_first(1, 3, yh)
    mi_c = push(MIS, MI.at[core], at_core)
    mo_c = push(MOS, MO.at[core], at_core)
    crossed(tc, "1")
    halve_first(0, 0, far)
    gather_cross(CA, cc, far, "1")
    for j in range(1, CHUNKS):
        halve_first(0, j, far)
    crossed(cc, "1")
    for j in range(CHUNKS):
        halve_first(1, j, far)
    for u in units:
        halve_second(0, *u)
    for u in units:
        halve_third(0, *u)
    for u in units:
        halve_second(1, *u)
    for u in parted:
        make_hidden(*u)
    for u in units:
        halve_third(1, *u)
    for u in parted:
        double_second(0, *u, H)
    for u in parted:
        make_grad(*u)
    for u in parted:
        double_third(0, *u, H)
    for u in parted:
        double_second(1, *u, G)

    every = slice(None)

    def out_part(A, p, k, weight, right_dim):
        left = jnp.concatenate([A[i, :, p].reshape(256, WIDE) for i in range(CHUNKS)], axis=1)
        R[k, p] = dot(left, weight[k], 1, right_dim).reshape(2, 2, 2, 2, 16, 512)

    def row_cross(n, p):
        return push(R.at[other, p], RX.at[n, p], at_core)

    def full(n, p, idx):
        return R[(core, p) + idx] + RX[(n, p) + idx]

    def row_first(cross, n, p):
        cross.wait_recv()
        T1[n, p, 0] = full(n, p, (1 - xb, every, every, 0)).astype(BF)
        a = push(T1.at[n, p, 0], U1.at[n, p, 0], at_xb)
        T1[n, p, 1] = full(n, p, (every, 1 - xa, every, 1)).astype(BF)
        b = push(T1.at[n, p, 1], U1.at[n, p, 1], at_xa)
        return a, b

    def row_second(copies, n, p):
        copies[0].wait_recv()
        T2[n, p, 0] = (full(n, p, (xb, every, every, 0)) + U1[n, p, 0].astype(F32)).astype(BF)
        KEEP[n, p, 0] = full(n, p, (xb, xa, yh, 0)) + U1[n, p, 0, xa, yh].astype(F32)
        copies[1].wait_recv()
        T2[n, p, 1] = (full(n, p, (every, xa, every, 1)) + U1[n, p, 1].astype(F32)).astype(BF)
        KEEP[n, p, 1] = full(n, p, (xb, xa, yh, 1)) + U1[n, p, 1, xb, yh].astype(F32)

    def row_direct(n, p):
        got = []
        for hf, mine, side, corner in ((0, xa, at_xa, at_xa_yh), (1, xb, at_xb, at_xb_yh)):
            got.append(push(T2.at[n, p, hf, 1 - mine, 1 - yh], U2.at[n, p, hf, 0], corner))
            got.append(push(T2.at[n, p, hf, mine, 1 - yh], U2.at[n, p, hf, 1], at_yh))
            got.append(push(T2.at[n, p, hf, 1 - mine, yh], U2.at[n, p, hf, 2], side))
        return got

    def result_second(copies, p):
        copies[0].wait_recv()
        T2[0, p, 0, 0] = (full(0, p, (xb, 1 - xa, every, 0)) + U1[0, p, 0, 1 - xa].astype(F32)).astype(BF)
        a = push(T2.at[0, p, 0, 0], U2.at[0, p, 0, pl.ds(0, 2)], at_xa)
        copies[1].wait_recv()
        T2[0, p, 1, 0] = (full(0, p, (1 - xb, xa, every, 1)) + U1[0, p, 1, 1 - xb].astype(F32)).astype(BF)
        b = push(T2.at[0, p, 1, 0], U2.at[0, p, 1, pl.ds(0, 2)], at_xb)
        return a, b

    def result_third(copies, p):
        def row_sum(v, hf):
            near = (xa, xb)[hf]
            return (
                full(0, p, (xb, xa, v, hf))
                + U1[0, p, hf, near, v].astype(F32)
                + U2[0, p, hf, v].astype(F32)
            )

        for hf in range(2):
            copies[hf].wait_recv()
            T2[0, p, hf, 1, 0] = row_sum(1 - yh, hf).astype(BF)
            KEEP[0, p, hf] = row_sum(yh, hf)

    def result_fourth(p):
        return push(T2.at[0, p, :, 1, 0], U2.at[0, p, :, 2], at_yh)

    def result_last(copy, p):
        copy.wait_recv()
        res_o[p] = (KEEP[0, p] + U2[0, p, :, 2].astype(F32)).astype(BF)

    def row_last(copies, n, p, out):
        for copy in copies:
            copy.wait_recv()
        total = KEEP[n, p]
        for k in range(3):
            total = total + U2[n, p, :, k].astype(F32)
        out[p] = total.astype(BF)

    def out_grad(k, to):
        def step(t, carry):
            j, c = lax.div(t, 2), pl.multiple_of(256 * lax.rem(t, 2), 256)
            left = H[j, :, :, :, pl.ds(c, 256)].reshape(768, 256)
            got = dot(left, CA[k].reshape(768, 512), 0, 0).reshape(2, 8, 16, 512)
            m = MO[k, pl.ds(2 * t, 2)].astype(F32)
            to(t, (got * m[:, None]).reshape(256, 512).astype(BF))
            return carry
        lax.fori_loop(0, 8, step, 0)

    def far_out(t, v):
        FO[pl.ds(pl.multiple_of(t * 256, 256), 256), :] = v

    def own_out(t, v):
        DO[pl.ds(pl.multiple_of(core * 2048 + t * 256, 256), 256), :] = v

    def in_grad(lo, hi, k, to):
        def step(i, carry):
            d = pl.multiple_of(i * 256, 256)
            left = TA[k, :, :, :, :, :, pl.ds(d, 256)].reshape(768, 256)
            for j in range(CHUNKS):
                got = dot(left, G[j].reshape(768, WIDE), 0, 0).reshape(2, 8, 16, WIDE)
                m = MI[k, pl.ds(2 * i, 2), :, WIDE * j : WIDE * (j + 1)].astype(F32)
                to(d, j, (got * m[:, None]).reshape(256, WIDE).astype(BF))
            return carry
        lax.fori_loop(lo, hi, step, 0)

    def far_in(d, j, v):
        FI[pl.ds(d, 256), WIDE * j : WIDE * (j + 1)] = v

    def own_in(d, j, v):
        DI[pl.ds(d, 256), pl.ds(pl.multiple_of(core * 2048 + WIDE * j, WIDE), WIDE)] = v

    def arrived(s, p):
        for j in range(CHUNKS):
            d3[s][j, p].wait_recv()

    cross0, cross1, pair0, pair1 = {}, {}, {}, {}

    def third_of(p):
        for j in range(CHUNKS):
            double_third(1, j, p, G)

    for p in range(PARTS):
        arrived(0, p)
        out_part(H, p, other, WO, 0)
        cross0[p] = row_cross(0, p)
        if p == 2:
            third_of(0)
        out_part(H, p, core, WO, 0)
    third_of(1)
    pair0[0] = row_first(cross0[0], 0, 0)
    third_of(2)
    for p in (1, 2):
        pair0[p] = row_first(cross0[p], 0, p)
    wo_c.wait_send()
    mo_c.wait_recv()
    out_grad(other, far_out)
    dwo_far = push(FO, DO.at[cols(core)], at_core)
    for p in range(PARTS):
        pair0[p] = result_second(pair0[p], p)
    out_grad(core, own_out)
    for p in range(PARTS):
        result_third(pair0[p], p)
        cross0[p].wait_send()

    def row_part(p):
        arrived(1, p)
        out_part(G, p, other, WI, 1)
        cross1[p] = row_cross(1, p)

    row_part(0)
    out_part(G, 0, core, WI, 1)
    row_part(1)
    pair1[0] = row_first(cross1[0], 1, 0)
    out_part(G, 1, core, WI, 1)
    row_part(2)
    last0 = [result_fourth(p) for p in range(PARTS)]
    pair1[1] = row_first(cross1[1], 1, 1)
    out_part(G, 2, core, WI, 1)
    last1 = []
    row_second(pair1[0], 1, 0)
    last1.append(row_direct(1, 0))
    pair1[2] = row_first(cross1[2], 1, 2)
    wi_c.wait_send()
    mi_c.wait_recv()
    in_grad(0, 1, other, far_in)
    row_second(pair1[1], 1, 1)
    last1.append(row_direct(1, 1))
    in_grad(1, 2, other, far_in)
    dwi_far = push(FI, DI.at[:, cols(core)], at_core)
    row_second(pair1[2], 1, 2)
    last1.append(row_direct(1, 2))
    in_grad(0, 2, core, own_in)
    for p in range(PARTS):
        result_last(last0[p], p)
    for p in range(PARTS):
        row_last(last1[p], 1, p, tg_o)
    dwo_far.wait_recv()
    dwi_far.wait_recv()
    waited = [wo_c, wi_c] + list(cross0.values())
    for c in sent:
        if not any(c is w for w in waited):
            c.wait_send()


def leave(a, b, c, d, a_o, b_o, c_o, d_o, sem):
    pairs = []
    for i in range(4):
        pairs.append((c.at[pl.ds(128 * i, 128)], c_o.at[pl.ds(128 * i, 128)]))
        pairs.append((d.at[pl.ds(1024 * i, 1024)], d_o.at[pl.ds(1024 * i, 1024)]))
    pairs += [(a, a_o), (b, b_o)]
    copies = [pltpu.make_async_copy(src, dst, sem.at[k]) for k, (src, dst) in enumerate(pairs)]
    for copy in copies:
        copy.start()
    for copy in copies:
        copy.wait()


def body(tokens, weight_in, mask_in, weight_out, mask_out, cotangent):
    anywhere = pl.BlockSpec(memory_space=pl.ANY)
    vmem = pl.BlockSpec(memory_space=pltpu.VMEM)
    smem = pl.BlockSpec(memory_space=pltpu.SMEM)

    def halving():
        return [
            pltpu.VMEM((CHUNKS, PARTS, 2, 2, 32, WIDE), BF),
            pltpu.VMEM((CHUNKS, PARTS, 2, 2, 32, WIDE), BF),
            pltpu.VMEM((CHUNKS, PARTS, 2, 2, 32, WIDE), F32),
            pltpu.VMEM((CHUNKS, PARTS, 2, 32, WIDE), BF),
            pltpu.VMEM((CHUNKS, PARTS, 2, 32, WIDE), BF),
            pltpu.VMEM((CHUNKS, PARTS, 32, WIDE), BF),
            pltpu.VMEM((CHUNKS, PARTS, 32, WIDE), BF),
        ]

    held = pl.pallas_call(
        kernel,
        out_shape=(
            OUT_KIND((PARTS, 2, 16, 512), BF),
            OUT_KIND((PARTS, 2, 16, 512), BF),
            OUT_KIND((512, 4096), BF),
            OUT_KIND((4096, 512), BF),
        ),
        in_specs=[anywhere] * 4 + [smem] * 2,
        out_specs=(vmem,) * 4,
        scratch_shapes=[
            pltpu.VMEM((2, 2, 2, 2, 2, 48, 512), BF),
            pltpu.VMEM((2, 2, 2, 2, 2, 48, 512), BF),
            pltpu.VMEM((2, 512, 2048), BF),
            pltpu.VMEM((2, 2048, 512), BF),
            pltpu.VMEM((512, 2048), BF),
            pltpu.VMEM((2048, 512), BF),
            pltpu.VMEM((4, 16, 2048), BF),
            pltpu.VMEM((2, 4, 16, 2048), BF),
            pltpu.VMEM((16, 16, 512), BF),
            pltpu.VMEM((2, 16, 16, 512), BF),
        ]
        + halving()
        + halving()
        + [
            pltpu.VMEM((CHUNKS, 8, PARTS, 32, WIDE), BF),
            pltpu.VMEM((CHUNKS, 8, PARTS, 32, WIDE), BF),
            pltpu.VMEM((2, PARTS, 2, 2, 2, 2, 16, 512), F32),
            pltpu.VMEM((2, PARTS, 2, 2, 2, 2, 16, 512), F32),
            pltpu.VMEM((2, PARTS, 2, 2, 2, 16, 512), BF),
            pltpu.VMEM((2, PARTS, 2, 2, 2, 16, 512), BF),
            pltpu.VMEM((2, PARTS, 2, 2, 2, 16, 512), BF),
            pltpu.VMEM((2, PARTS, 2, 3, 16, 512), BF),
            pltpu.VMEM((2, PARTS, 2, 16, 512), F32),
            pltpu.SemaphoreType.DMA((N_COPIES,)),
            pltpu.SemaphoreType.DMA((N_COPIES,)),
            pltpu.SemaphoreType.DMA((8,)),
        ],
        compiler_params=pltpu.CompilerParams(
            collective_id=0, has_side_effects=True, vmem_limit_bytes=VMEM_BYTES
        ),
    )(tokens.reshape(2, 48, 512), cotangent.reshape(2, 48, 512), weight_in, weight_out, mask_in, mask_out.T)
    shapes = ((PARTS, 2, 16, 512), (PARTS, 2, 16, 512), (512, 4096), (4096, 512))
    result, tokens_grad, dwi, dwo = pl.pallas_call(
        leave,
        out_shape=tuple(jax.ShapeDtypeStruct(shape, BF) for shape in shapes),
        in_specs=[anywhere] * 4,
        out_specs=(anywhere,) * 4,
        scratch_shapes=[pltpu.SemaphoreType.DMA((10,))],
        compiler_params=pltpu.CompilerParams(vmem_limit_bytes=1024 * 1024),
    )(*held)
    return result.reshape(96, 512), tokens_grad.reshape(96, 512), dwi, dwo


def solution(mesh):
    return jax.shard_map(
        body,
        mesh=mesh,
        in_specs=(
            P("row", "col"),
            P("col", "row"),
            P("col", "row"),
            P("row", "col"),
            P("row", "col"),
            P("row", "col"),
        ),
        out_specs=(P("row", "col"), P("row", "col"), P("col", "row"), P("row", "col")),
        check_vma=False,
    )
```
